512 devices in a mesh: row: 2 (over core), ax: 8 (over x, z_lo), az: 32 (over z_hi, y).
Axes of the slice: x: 4, y: 8, z: 8 (z_hi: 4, z_lo: 2; z = z_hi * 2 + z_lo), core: 2. Of those that a mesh axis runs over, the one named last changes fastest.
Arguments:
- density: float32 [2, 16, 1024, 512], P('row', 'ax', 'az'), may hold values from 0.8 to 1.6
- velocity: float32 [2, 3, 16, 1024, 512], P('row', None, 'ax', 'az'), may hold values from -1.5 to 1.5
- pressure: float32 [2, 16, 1024, 512], P('row', 'ax', 'az'), may hold values from 0.4 to 1.2
- offsets: int32 [3], replicated, may hold values from 0 to 1023
Outputs:
- final_state: float32 [2, 5, 16, 1024, 512], P('row', None, 'ax', 'az')
The draws below stay inside these ranges and needn't reach their ends.
All inputs are finite; a program needn't handle non-finite values.
Results may differ from the reference program's by a relative error of at most 0.00002.
Values sent between devices are 32-bit elements; how exact they have to be, the bound alone decides.
No kernel may reach another device: no remote copies, remote signals or barrier semaphores. Data moves between devices by JAX's collectives and lax.ppermute only.
A program may use at most 128 MiB of HBM per device.

```python
import math
import jax
import jax.numpy as jnp
from jax import lax

CR = 512
SUBSTEPS = 3
NT = 1024
NZ = 16


def draw_velocity(key, part):
    noise_key = jax.random.fold_in(key, 11)
    phase_key = jax.random.fold_in(key, 12)
    size_key = jax.random.fold_in(key, 13)
    noise_field = jnp.clip(0.3 * jax.random.normal(noise_key, (2, 3, NZ, NT, CR), jnp.float32), -1.2, 1.2)
    phase_shift = jax.random.randint(phase_key, (2, 1, NZ, 1, 1), 0, 4)
    azimuth = jnp.arange(NT, dtype=jnp.int32).reshape(1, 1, 1, NT, 1)
    sign_pattern = jnp.where((azimuth + phase_shift) % 4 < 2, 1.0, -1.0).astype(jnp.float32)
    magnitude = 1.2 + 0.3 * jax.random.uniform(size_key, (2, 1, NZ, NT, CR), jnp.float32)
    radial_index = jnp.arange(CR, dtype=jnp.int32).reshape(1, 1, 1, 1, CR)
    component = jnp.arange(3, dtype=jnp.int32).reshape(1, 3, 1, 1, 1)
    inner_band = (radial_index < CR // 4) & (component == 1)
    return jnp.where(inner_band, sign_pattern * magnitude, noise_field).astype(jnp.float32)


def level_of(key, dims, split, low, high):
    gain = 1.0
    for position, parts in split:
        draws = jax.random.uniform(jax.random.fold_in(jax.random.fold_in(key, 6), position), (parts,), jnp.float32, low / len(split), high / len(split))
        gain = gain * jnp.repeat(jnp.exp(draws), dims[position] // parts).reshape((-1,) + (1,) * (len(dims) - 1 - position))
    return gain


def setup_inputs(seed: int = 0) -> dict:
    streams_of = jax.random.split(jax.random.key(seed), 5)
    return {
        "density": jnp.clip(0.8 + 0.8 * jax.random.uniform(streams_of[0], (2, NZ, NT, CR), jnp.float32) ** level_of(streams_of[0], (2, NZ, NT, CR), ((0, 2), (1, 8), (2, 32)), -0.2, 0.2), 0.8, 1.6),
        "velocity": draw_velocity(jax.random.fold_in(streams_of[4], 71), 0),
        "pressure": jnp.clip(0.4 + 0.800000042 * jax.random.uniform(streams_of[2], (2, NZ, NT, CR), jnp.float32) ** level_of(streams_of[2], (2, NZ, NT, CR), ((0, 2), (1, 8), (2, 32)), -0.2, 0.2), 0.4, 1.2),
        "offsets": jax.random.randint(streams_of[3], (SUBSTEPS,), 0, NT).astype(jnp.int32),
    }


HEAT_RATIO = 1.4
VISCOSITY = 0.8
CONDUCTION = 0.6
TIME_STEP = 0.1
AXIAL_FLUX = 1.0
AXIAL_CURVE = 4.0


def conserved(density, velocity, pressure):
    momentum = density[:, None] * velocity
    energy = pressure / (HEAT_RATIO - 1.0) + 0.5 * density * jnp.sum(velocity * velocity, axis=1)
    return jnp.concatenate([density[:, None], momentum, energy[:, None]], axis=1)


def primitive(state):
    vel_theta = state[:, 1] / state[:, 0]
    vel_radial = state[:, 2] / state[:, 0]
    vel_axial = state[:, 3] / state[:, 0]
    press = (HEAT_RATIO - 1.0) * (state[:, 4] - 0.5 * (state[:, 1] * vel_theta + state[:, 2] * vel_radial + state[:, 3] * vel_axial))
    return (vel_theta, vel_radial, vel_axial, press / state[:, 0], press)


def fluxes(state, values, direction):
    normal_vel = values[direction]
    press = values[4]
    flux_terms = [state[:, 0] * normal_vel, state[:, 1] * normal_vel, state[:, 2] * normal_vel, state[:, 3] * normal_vel, (state[:, 4] + press) * normal_vel]
    flux_terms[1 + direction] = flux_terms[1 + direction] + press
    return flux_terms


def laplace(center, theta_lo, theta_hi, radial_lo, radial_hi, axial_lo, axial_hi, radius, dtheta):
    beside_all = (theta_hi - 2.0 * center + theta_lo) / (radius * dtheta) ** 2
    across = ((radius + 0.5) * (radial_hi - center) - (radius - 0.5) * (center - radial_lo)) / radius
    return beside_all + across + AXIAL_CURVE * (axial_hi - 2.0 * center + axial_lo)


def tendency(center, theta_lo, theta_hi, radial_lo, radial_hi, axial_lo, axial_hi, radius, dtheta):
    values_c = primitive(center)
    values_tl = primitive(theta_lo)
    values_th = primitive(theta_hi)
    values_rl = primitive(radial_lo)
    values_rh = primitive(radial_hi)
    values_zl = primitive(axial_lo)
    values_zh = primitive(axial_hi)
    flux_tl = fluxes(theta_lo, values_tl, 0)
    flux_th = fluxes(theta_hi, values_th, 0)
    flux_rl = fluxes(radial_lo, values_rl, 1)
    flux_rh = fluxes(radial_hi, values_rh, 1)
    flux_zl = fluxes(axial_lo, values_zl, 2)
    flux_zh = fluxes(axial_hi, values_zh, 2)
    result = []
    for field_index in range(5):
        divergence = -(flux_th[field_index] - flux_tl[field_index]) / (2.0 * radius * dtheta)
        divergence = divergence - ((radius + 1.0) * flux_rh[field_index] - (radius - 1.0) * flux_rl[field_index]) / (2.0 * radius)
        divergence = divergence - AXIAL_FLUX * (flux_zh[field_index] - flux_zl[field_index])
        result.append(divergence)

    def viscous(which):
        return laplace(values_c[which], values_tl[which], values_th[which], values_rl[which], values_rh[which], values_zl[which], values_zh[which], radius, dtheta)

    density_now = center[:, 0]
    result[1] = result[1] - density_now * values_c[0] * values_c[1] / radius + VISCOSITY * (viscous(0) - values_c[0] / radius ** 2 + (values_th[1] - values_tl[1]) / (radius ** 2 * dtheta))
    result[2] = result[2] + (density_now * values_c[0] * values_c[0] + values_c[4]) / radius + VISCOSITY * (viscous(1) - values_c[1] / radius ** 2 - (values_th[0] - values_tl[0]) / (radius ** 2 * dtheta))
    result[3] = result[3] + VISCOSITY * viscous(2)
    result[4] = result[4] + CONDUCTION * viscous(3)
    return jnp.stack(result, axis=1)


def full_rate(state, shift, radius, dtheta):
    axial_sign = jnp.array([1.0, 1.0, 1.0, -1.0, 1.0], dtype=jnp.float32).reshape(5, 1, 1)
    wall_sign = jnp.array([1.0, -1.0, -1.0, -1.0, 1.0], dtype=jnp.float32).reshape(5, 1, 1)
    top_plane = state[:, :, -1] * axial_sign
    partner = top_plane[::-1]
    ghost_rotor = jnp.roll(partner[0], -shift, axis=1)
    ghost_stator = jnp.roll(partner[1], shift, axis=1)
    upper_ghost = jnp.stack([ghost_rotor, ghost_stator])[:, :, None]
    padded = jnp.concatenate([state[:, :, :1], state, upper_ghost], axis=2)

    def plane_rate(section):
        plane_block = lax.dynamic_slice_in_dim(padded, section, 3, 2)
        center = plane_block[:, :, 1]
        theta_lo = jnp.roll(center, 1, axis=2)
        theta_hi = jnp.roll(center, -1, axis=2)
        radial_lo = jnp.concatenate([center[..., :1] * wall_sign, center[..., :-1]], axis=3)
        radial_hi = jnp.concatenate([center[..., 1:], center[..., -1:] * wall_sign], axis=3)
        return tendency(center, theta_lo, theta_hi, radial_lo, radial_hi, plane_block[:, :, 0], plane_block[:, :, 2], radius, dtheta)

    planes = lax.map(plane_rate, jnp.arange(NZ, dtype=jnp.int32))
    return jnp.moveaxis(planes, 0, 2)


def reference(density, velocity, pressure, offsets):
    dtheta = 2.0 * math.pi / NT
    radius = NT / (2.0 * math.pi) + jnp.arange(CR, dtype=jnp.float32) + 0.5
    state0 = conserved(density, velocity, pressure)
    state1 = state0 + TIME_STEP * full_rate(state0, offsets[0], radius, dtheta)
    state2 = 0.75 * state0 + 0.25 * (state1 + TIME_STEP * full_rate(state1, offsets[1], radius, dtheta))
    return state0 / 3.0 + (2.0 / 3.0) * (state2 + TIME_STEP * full_rate(state2, offsets[2], radius, dtheta))
```

```python
import math

import jax
import jax.numpy as jnp
from jax import lax
from jax.experimental import pallas as pl
from jax.experimental.pallas import tpu as pltpu
from jax.sharding import PartitionSpec as P

HEAT_RATIO = 1.4
VISCOSITY = 0.8
CONDUCTION = 0.6
TIME_STEP = 0.1
AXIAL_CURVE = 4.0
AXES = ("row", "ax", "az")
FIELDS = 5
SUB = 8


def cell(state):
    rho, mt, mr, mz, energy = state
    inv = 1.0 / rho
    vt, vr, vz = mt * inv, mr * inv, mz * inv
    tt, rr, zz = mt * vt, mr * vr, mz * vz
    press = (HEAT_RATIO - 1.0) * (energy - 0.5 * (tt + rr + zz))
    enth = energy + press
    visc = (
        None,
        VISCOSITY * vt,
        VISCOSITY * vr,
        VISCOSITY * vz,
        CONDUCTION * (press * inv),
    )
    return dict(
        mt=mt, mr=mr, mz=mz, vt=vt, vr=vr, vz=vz, tt=tt, rr=rr, zz=zz,
        tr=mt * vr, tz=mt * vz, rz=mr * vz, press=press, enth=enth, visc=visc,
    )


def flux_theta(c):
    return (c["mt"], c["tt"] + c["press"], c["tr"], c["tz"], c["enth"] * c["vt"])


def flux_radial(c):
    return (c["mr"], c["tr"], c["rr"] + c["press"], c["rz"], c["enth"] * c["vr"])


def flux_axial(c):
    return (c["mz"], c["tz"], c["rz"], c["zz"] + c["press"], c["enth"] * c["vz"])


def axial_terms(c, to_above):
    out = []
    for flux, visc in zip(flux_axial(c), c["visc"]):
        term = flux if to_above else -flux
        out.append(term if visc is None else term + AXIAL_CURVE * visc)
    return out


def theta_terms(c, co):
    flux = [co["half_arc"] * f for f in flux_theta(c)]
    flux[1] = flux[1] - co["cross"] * c["visc"][2]
    flux[2] = flux[2] + co["cross"] * c["visc"][1]
    nxt, prv = [flux[0]], [-flux[0]]
    for k in range(1, FIELDS):
        side = co["arc2"] * c["visc"][k]
        nxt.append(side + flux[k])
        prv.append(side - flux[k])
    return nxt, prv


def radial_terms(c, co):
    out, inn = [], []
    for flux, visc in zip(flux_radial(c), c["visc"]):
        odd = co["half_r"] * flux
        if visc is None:
            out.append(odd)
            inn.append(-odd)
        else:
            odd = odd + 0.5 * visc
            even = co["r"] * visc
            out.append(even + odd)
            inn.append(even - odd)
    return out, inn


def wall_terms(c, half_rg, weight, sign):
    flux = flux_radial(c)
    signs = (-1.0, 1.0, 1.0, 1.0, -1.0)
    out = []
    for k in range(FIELDS):
        term = (sign * signs[k]) * (half_rg * flux[k])
        if k:
            term = term + (1.0 if k == 4 else -1.0) * (weight * c["visc"][k])
        out.append(term)
    return out


def centre_terms(c, co):
    centre = [None] + [-(co["centre"] * v) for v in c["visc"][1:]]
    centre[1] = centre[1] - co["inv_r"] * (c["tr"] + co["inv_r"] * c["visc"][1])
    centre[2] = centre[2] + co["inv_r"] * (c["tt"] + c["press"] - co["inv_r"] * c["visc"][2])
    return centre


COEFS = ("r", "half_r", "inv_r", "half_arc", "arc2", "cross", "centre", "pad")


def coefficient_rows(cells, cycle_cells):
    dtheta = 2.0 * math.pi / cycle_cells
    r = cycle_cells / (2.0 * math.pi) + jnp.arange(cells, dtype=jnp.float32) + 0.5
    arc2 = 1.0 / (r * dtheta) ** 2
    rows = [
        r, 0.5 * r, 1.0 / r, 1.0 / (2.0 * r * dtheta), arc2,
        1.0 / (r**2 * dtheta), 2.0 * arc2 + 2.0 + 2.0 * AXIAL_CURVE, jnp.zeros_like(r),
    ]
    return jnp.stack(rows)


def load_coefs(co_ref):
    return {name: co_ref[i : i + 1, :] for i, name in enumerate(COEFS)}


def write_sends(states, co, b, blocks, up_ref, dn_ref, nxt_ref, prv_ref):
    rows = pl.ds(b * SUB, SUB)
    cells = [cell(s) for s in states]
    for k, term in enumerate(axial_terms(cells[1], True)):
        up_ref[k, rows, :] = term
    for k, term in enumerate(axial_terms(cells[0], False)):
        dn_ref[k, rows, :] = term
    if b == 0 or b == blocks - 1:
        for p in range(2):
            nxt, prv = theta_terms(cells[p], co)
            for k in range(FIELDS):
                if b == 0:
                    prv_ref[2 * k + p : 2 * k + p + 1, :] = prv[k][0:1, :]
                if b == blocks - 1:
                    nxt_ref[2 * k + p : 2 * k + p + 1, :] = nxt[k][SUB - 1 : SUB, :]


def first_kernel(rho_ref, vel_ref, press_ref, co_ref, state_ref, up_ref, dn_ref, nxt_ref, prv_ref):
    co = load_coefs(co_ref)
    blocks = rho_ref.shape[1] // SUB
    for b in range(blocks):
        rows = pl.ds(b * SUB, SUB)
        states = []
        for p in range(2):
            rho = rho_ref[p, rows, :]
            vel = [vel_ref[d, p, rows, :] for d in range(3)]
            square = vel[0] * vel[0] + vel[1] * vel[1] + vel[2] * vel[2]
            energy = press_ref[p, rows, :] / (HEAT_RATIO - 1.0) + 0.5 * rho * square
            state = [rho] + [rho * v for v in vel] + [energy]
            for k in range(FIELDS):
                state_ref[k, p, rows, :] = state[k]
            states.append(state)
        write_sends(states, co, b, blocks, up_ref, dn_ref, nxt_ref, prv_ref)


def local_kernel(weights, flag_ref, *refs):
    old_w, now_w, rate_w = weights
    if old_w:
        old_ref, refs = refs[0], refs[1:]
    now_ref, co_ref, base_ref, nxt_s, prv_s = refs
    co = load_coefs(co_ref)
    lanes = now_ref.shape[3]
    blocks = now_ref.shape[2] // SUB
    at_outer = flag_ref[0] == 1
    lane = lax.broadcasted_iota(jnp.int32, (SUB, lanes), 1)
    is_inner, is_outer = lane == 0, lane == lanes - 1
    low_half, low_weight = 0.5 * (co["r"] - 1.0), co["r"] - 0.5
    high_half, high_weight = 0.5 * (co["r"] + 1.0), co["r"] + 0.5
    zero_row = jnp.zeros((SUB, lanes), jnp.float32)
    for k in range(FIELDS):
        for p in range(2):
            nxt_s[k, p, pl.ds(0, SUB), :] = zero_row
            prv_s[k, p, pl.ds(blocks * SUB, SUB), :] = zero_row
    for b in range(blocks):
        rows = pl.ds(b * SUB, SUB)
        for p in range(2):
            here = cell([now_ref[k, p, rows, :] for k in range(FIELDS)])
            other = cell([now_ref[k, 1 - p, rows, :] for k in range(FIELDS)])
            axial = axial_terms(other, p == 1)
            if p == 0:
                below = axial_terms(here, True)
                axial = [a + jnp.where(at_outer, z, 0.0) for a, z in zip(axial, below)]
            to_out, to_in = radial_terms(here, co)
            low = wall_terms(here, low_half, low_weight, 1.0)
            high = wall_terms(here, high_half, high_weight, -1.0)
            centre = centre_terms(here, co)
            nxt, prv = theta_terms(here, co)
            for k in range(FIELDS):
                inside = jnp.where(is_inner, low[k], pltpu.roll(to_out[k], 1, 1))
                outside = jnp.where(is_outer, high[k], pltpu.roll(to_in[k], lanes - 1, 1))
                total = axial[k] + co["inv_r"] * (inside + outside)
                if centre[k] is not None:
                    total = total + centre[k]
                base_ref[k, p, rows, :] = total
                nxt_s[k, p, pl.ds(b * SUB + SUB, SUB), :] = nxt[k]
                prv_s[k, p, rows, :] = prv[k]
    for b in range(blocks):
        rows = pl.ds(b * SUB, SUB)
        for p in range(2):
            for k in range(FIELDS):
                rate = (
                    base_ref[k, p, rows, :]
                    + nxt_s[k, p, pl.ds(b * SUB + SUB - 1, SUB), :]
                    + prv_s[k, p, pl.ds(b * SUB + 1, SUB), :]
                )
                value = now_w * now_ref[k, p, rows, :] + rate_w * rate
                if old_w:
                    value = value + old_w * old_ref[k, p, rows, :]
                base_ref[k, p, rows, :] = value


def join_kernel(rate_w, last, flag_ref, base_ref, below_ref, above_ref, turn_ref, turn2_ref,
                nxt_ref, prv_ref, co_ref, state_ref, *sends):
    co = load_coefs(co_ref)
    blocks = base_ref.shape[2] // SUB
    lanes = base_ref.shape[3]
    split, flip, shift = flag_ref[1], flag_ref[2], flag_ref[3]
    rows_all = blocks * SUB
    row_id = lax.broadcasted_iota(jnp.int32, (rows_all, lanes), 0)
    from_first = (row_id >= split) != (flip == 1)
    row8 = lax.broadcasted_iota(jnp.int32, (SUB, lanes), 0)
    for k in range(FIELDS):
        mixed = jnp.where(from_first, turn_ref[k], turn2_ref[k])
        turned = pltpu.roll(mixed, shift, 0)
        upper = above_ref[k] + (-turned if k == 3 else turned)
        for p in range(2):
            add = upper if p == 1 else below_ref[k]
            state_ref[k, p] = base_ref[k, p] + rate_w * add
            first = state_ref[k, p, pl.ds(0, SUB), :]
            row = nxt_ref[2 * k + p : 2 * k + p + 1, :]
            state_ref[k, p, pl.ds(0, SUB), :] = first + jnp.where(row8 == 0, rate_w * row, 0.0)
            end = pl.ds((blocks - 1) * SUB, SUB)
            final = state_ref[k, p, end, :]
            row = prv_ref[2 * k + p : 2 * k + p + 1, :]
            state_ref[k, p, end, :] = final + jnp.where(row8 == SUB - 1, rate_w * row, 0.0)
    if last:
        return
    for b in range(blocks):
        rows = pl.ds(b * SUB, SUB)
        states = [[state_ref[k, p, rows, :] for k in range(FIELDS)] for p in range(2)]
        write_sends(states, co, b, blocks, *sends)


def body(density, velocity, pressure, offsets):
    sizes = {name: lax.axis_size(name) for name in AXES}
    n_ax, n_az = sizes["ax"], sizes["az"]
    planes, tile, cells = density.shape[1:]
    cycle_cells = tile * n_az
    coefs = coefficient_rows(cells, cycle_cells)
    is_rotor = lax.axis_index("row") == 0
    at_outer = lax.axis_index("ax") == 0

    vmem = pl.BlockSpec(memory_space=pltpu.VMEM)
    smem = pl.BlockSpec(memory_space=pltpu.SMEM)
    block = jax.ShapeDtypeStruct((FIELDS, planes, tile, cells), jnp.float32)
    plane = jax.ShapeDtypeStruct((FIELDS, tile, cells), jnp.float32)
    edge = jax.ShapeDtypeStruct((FIELDS * planes, cells), jnp.float32)
    sends = (plane, plane, edge, edge)

    def device(row, ax, az):
        return (row * n_ax + ax) * n_az + az

    def along_az(by):
        return [
            (device(row, ax, az), device(row, ax, (az + by) % n_az))
            for row in range(2) for ax in range(n_ax) for az in range(n_az)
        ]

    def along_ax(by):
        return [
            (device(row, ax, az), device(row, ax + by, az))
            for row in range(2) for ax in range(n_ax) for az in range(n_az)
            if 0 <= ax + by < n_ax
        ]

    def turned(by):
        top = n_ax - 1
        pairs = []
        for az in range(n_az):
            pairs.append((device(1, top, (az + by) % n_az), device(0, top, az)))
            pairs.append((device(0, top, az), device(1, top, (az + by) % n_az)))
        return pairs

    def turn(up, offset):
        def branch(by):
            def run(value):
                return (
                    lax.ppermute(value, AXES, turned(by)),
                    lax.ppermute(value, AXES, turned((by + 1) % n_az)),
                )
            return run
        return lax.switch(offset // tile, [branch(by) for by in range(n_az)], up)

    def call(kernel, outs, n_in, flags=True, scratch=()):
        specs = [vmem] * n_in
        if flags:
            specs = [smem] + specs
        return pl.pallas_call(
            kernel,
            out_shape=outs,
            in_specs=specs,
            out_specs=jax.tree.map(lambda _: vmem, outs),
            scratch_shapes=list(scratch),
            cost_estimate=pl.CostEstimate(flops=8_000_000, bytes_accessed=3_000_000, transcendentals=0),
        )

    taller = pltpu.VMEM((FIELDS, planes, tile + SUB, cells), jnp.float32)
    state, up, dn, nxt, prv = call(first_kernel, (block, *sends), 4, flags=False)(
        density[0], velocity[0], pressure[0], coefs
    )
    old = state
    plans = ((0.0, 1.0, 1.0), (0.75, 0.25, 0.25), (1.0 / 3.0, 2.0 / 3.0, 2.0 / 3.0))
    for step, (old_w, now_w, rate_w) in enumerate(plans):
        rate_w = rate_w * TIME_STEP
        last = step == len(plans) - 1
        offset = offsets[step]
        rest = offset % tile
        flags = jnp.stack([
            at_outer.astype(jnp.int32),
            jnp.where(is_rotor, rest, tile - rest),
            jnp.where(is_rotor, 0, 1),
            jnp.where(is_rotor, (tile - rest) % tile, rest),
        ]).astype(jnp.int32)
        from_prev = lax.ppermute(nxt, AXES, along_az(1))
        from_next = lax.ppermute(prv, AXES, along_az(-1))
        below = lax.ppermute(up, AXES, along_ax(1))
        above = lax.ppermute(dn, AXES, along_ax(-1))
        turn1, turn2 = turn(up, offset)
        kernel = lambda *refs, w=(old_w, now_w, rate_w): local_kernel(w, *refs)
        operands = ((old,) if old_w else ()) + (state, coefs)
        base = call(kernel, block, len(operands), scratch=(taller, taller))(flags, *operands)
        kernel = lambda *refs, w=rate_w, end=last: join_kernel(w, end, *refs)
        outs = block if last else (block, *sends)
        result = call(kernel, outs, 8)(
            flags, base, below, above, turn1, turn2, from_prev, from_next, coefs
        )
        if last:
            return result[None]
        state, up, dn, nxt, prv = result


def solution(mesh):
    placed = (
        P("row", "ax", "az", None),
        P("row", None, "ax", "az", None),
        P("row", "ax", "az", None),
        P(),
    )
    return jax.shard_map(
        body,
        mesh=mesh,
        in_specs=placed,
        out_specs=P("row", None, "ax", "az", None),
        check_vma=False,
    )
```

```python
import functools
import math

import jax
import jax.numpy as jnp
from jax import lax
from jax.experimental import pallas as pl
from jax.experimental.pallas import tpu as pltpu
from jax.sharding import PartitionSpec as P

HEAT_RATIO = 1.4
VISCOSITY = 0.8
CONDUCTION = 0.6
TIME_STEP = 0.1
AXIAL_CURVE = 4.0
AXES = ("row", "ax", "az")
FIELDS = 5
SUB = 8
LANES = 128
HALF = 64
IN_BRANCH = True
LOOP = True


def cell(state):
    rho, mt, mr, mz, energy = state
    inv = 1.0 / rho
    vt, vr, vz = mt * inv, mr * inv, mz * inv
    tt, rr, zz = mt * vt, mr * vr, mz * vz
    press = (HEAT_RATIO - 1.0) * (energy - 0.5 * (tt + rr + zz))
    visc = (
        None,
        VISCOSITY * vt,
        VISCOSITY * vr,
        VISCOSITY * vz,
        CONDUCTION * (press * inv),
    )
    return dict(
        mt=mt, mr=mr, mz=mz, vt=vt, vr=vr, vz=vz, tt=tt, rr=rr, zz=zz,
        tr=mt * vr, tz=mt * vz, rz=mr * vz, press=press, enth=energy + press, visc=visc,
    )


def flux_theta(c):
    return (c["mt"], c["tt"] + c["press"], c["tr"], c["tz"], c["enth"] * c["vt"])


def flux_radial(c):
    return (c["mr"], c["tr"], c["rr"] + c["press"], c["rz"], c["enth"] * c["vr"])


def flux_axial(c):
    return (c["mz"], c["tz"], c["rz"], c["zz"] + c["press"], c["enth"] * c["vz"])


def axial_terms(c):
    above, below = [], []
    for flux, visc in zip(flux_axial(c), c["visc"]):
        if visc is None:
            above.append(flux)
            below.append(-flux)
        else:
            side = AXIAL_CURVE * visc
            above.append(side + flux)
            below.append(side - flux)
    return above, below


def theta_terms(c, co):
    flux = [co["half_arc"] * f for f in flux_theta(c)]
    flux[1] = flux[1] - co["cross"] * c["visc"][2]
    flux[2] = flux[2] + co["cross"] * c["visc"][1]
    nxt, prv = [flux[0]], [-flux[0]]
    for k in range(1, FIELDS):
        side = co["arc2"] * c["visc"][k]
        nxt.append(side + flux[k])
        prv.append(side - flux[k])
    return nxt, prv


def radial_terms(c, co):
    out, inn = [], []
    for flux, visc in zip(flux_radial(c), c["visc"]):
        odd = co["half_r"] * flux
        if visc is None:
            out.append(odd)
            inn.append(-odd)
        else:
            odd = odd + 0.5 * visc
            even = co["r"] * visc
            out.append(even + odd)
            inn.append(even - odd)
    return out, inn


def wall_terms(c, half_rg, weight, sign):
    flux = flux_radial(c)
    signs = (-1.0, 1.0, 1.0, 1.0, -1.0)
    out = []
    for k in range(FIELDS):
        term = (sign * signs[k]) * (half_rg * flux[k])
        if k:
            term = term + (1.0 if k == 4 else -1.0) * (weight * c["visc"][k])
        out.append(term)
    return out


def centre_terms(c, co):
    centre = [None] + [-(co["centre"] * v) for v in c["visc"][1:]]
    centre[1] = centre[1] - co["inv_r"] * (c["tr"] + co["inv_r"] * c["visc"][1])
    centre[2] = centre[2] + co["inv_r"] * (c["tt"] + c["press"] - co["inv_r"] * c["visc"][2])
    return centre


def lanes_of():
    lane = lax.broadcasted_iota(jnp.int32, (SUB, LANES), 1)
    return lane, jnp.where(lane < HALF, lane, lane - HALF)


def coefficients(segment, cycle_cells):
    dtheta = 2.0 * math.pi / cycle_cells
    cells = (lanes_of()[1] + segment * HALF).astype(jnp.float32)
    r = cycle_cells / (2.0 * math.pi) + cells + 0.5
    inv_r = 1.0 / r
    arc2 = 1.0 / ((r * dtheta) * (r * dtheta))
    return dict(
        r=r, half_r=0.5 * r, inv_r=inv_r, half_arc=1.0 / (2.0 * r * dtheta), arc2=arc2,
        cross=1.0 / (r * r * dtheta), centre=2.0 * arc2 + 2.0 + 2.0 * AXIAL_CURVE,
    )


def pack_kernel(rho_ref, vel_ref, press_ref, out_ref):
    lane, _ = lanes_of()
    low = lane < HALF
    for b in range(rho_ref.shape[1] // SUB):
        rows = pl.ds(b * SUB, SUB)
        for w in range(rho_ref.shape[2] // LANES):
            cols = pl.ds(w * LANES, LANES)
            both = []
            for p in range(2):
                rho = rho_ref[p, rows, cols]
                vel = [vel_ref[d, p, rows, cols] for d in range(3)]
                square = vel[0] * vel[0] + vel[1] * vel[1] + vel[2] * vel[2]
                energy = press_ref[p, rows, cols] / (HEAT_RATIO - 1.0) + 0.5 * rho * square
                both.append([rho] + [rho * v for v in vel] + [energy])
            for k in range(FIELDS):
                first, second = both[0][k], both[1][k]
                out_ref[2 * w, k, rows, :] = jnp.where(low, first, pltpu.roll(second, HALF, 1))
                out_ref[2 * w + 1, k, rows, :] = jnp.where(low, pltpu.roll(first, HALF, 1), second)


def unpack_kernel(in_ref, out_ref):
    lane, _ = lanes_of()
    low = lane < HALF
    for b in range(in_ref.shape[2] // SUB):
        rows = pl.ds(b * SUB, SUB)
        for w in range(in_ref.shape[0] // 2):
            cols = pl.ds(w * LANES, LANES)
            for k in range(FIELDS):
                inner, outer = in_ref[2 * w, k, rows, :], in_ref[2 * w + 1, k, rows, :]
                out_ref[k, 0, rows, cols] = jnp.where(low, inner, pltpu.roll(outer, HALF, 1))
                out_ref[k, 1, rows, cols] = jnp.where(low, pltpu.roll(inner, HALF, 1), outer)


def write_sends(state_ref, co, up_ref, nxt_ref, prv_ref, out_ref, inn_ref):
    lane, place = lanes_of()
    pairs = state_ref.shape[0]
    blocks = state_ref.shape[2] // SUB
    top = []
    for b in range(blocks):
        rows = pl.ds(b * SUB, SUB)
        packed_out = jnp.zeros((SUB, LANES), jnp.float32)
        packed_in = jnp.zeros((SUB, LANES), jnp.float32)
        for a in range(pairs):
            c = cell([state_ref[a, k, rows, :] for k in range(FIELDS)])
            to_out, to_in = radial_terms(c, co)
            for k in range(FIELDS):
                j = a * FIELDS + k
                here = place == j
                moved = pltpu.roll(to_out[k], (j + 1 - HALF) % LANES, 1)
                packed_out = jnp.where(here, moved, packed_out)
                moved = pltpu.roll(to_in[k], j, 1) if j else to_in[k]
                packed_in = jnp.where(here, moved, packed_in)
            if b == 0 or b == blocks - 1:
                nxt, prv = theta_terms(c, co)
                for k in range(FIELDS):
                    j = a * FIELDS + k
                    if b == 0:
                        prv_ref[j : j + 1, :] = prv[k][0:1, :]
                    if b == blocks - 1:
                        nxt_ref[j : j + 1, :] = nxt[k][SUB - 1 : SUB, :]
            if a == pairs - 1:
                top.append(axial_terms(c)[0])
        out_ref[rows, :] = packed_out
        inn_ref[rows, :] = packed_in
    for b in range(blocks // 2):
        for k in range(FIELDS):
            up_ref[k, pl.ds(b * SUB, SUB), :] = jnp.where(
                lane < HALF, pltpu.roll(top[b][k], HALF, 1), top[b + blocks // 2][k]
            )


def first_kernel(cycle_cells, flag_ref, state_ref, *sends):
    co = coefficients(flag_ref[0], cycle_cells)
    write_sends(state_ref, co, *sends)


def local_kernel(cycle_cells, flag_ref, weight_ref, old_ref, now_ref, base_ref, nxt_s, prv_s, up_s, dn_s):
    segment, segments = flag_ref[0], flag_ref[1]
    co = coefficients(segment, cycle_cells)
    lane, place = lanes_of()
    low = lane < HALF
    pairs = now_ref.shape[0]
    blocks = now_ref.shape[2] // SUB
    at_inner, at_outer = segment == 0, segment == segments - 1
    is_inner, is_outer = place == 0, place == HALF - 1
    low_half, low_weight = 0.5 * (co["r"] - 1.0), co["r"] - 0.5
    high_half, high_weight = 0.5 * (co["r"] + 1.0), co["r"] + 0.5
    zero = jnp.zeros((SUB, LANES), jnp.float32)
    low_half = jnp.where(at_inner, low_half, zero)
    low_weight = jnp.where(at_inner, low_weight, zero)
    high_half = jnp.where(at_outer, high_half, zero)
    high_weight = jnp.where(at_outer, high_weight, zero)
    rows_end = blocks * SUB
    for k in range(FIELDS):
        nxt_s[k, pl.ds(0, SUB), :] = zero
        prv_s[k, pl.ds(rows_end, SUB), :] = zero

    def pair(a, carry):
        for b in range(blocks):
            rows = pl.ds(b * SUB, SUB)
            c = cell([now_ref[a, k, rows, :] for k in range(FIELDS)])
            to_out, to_in = radial_terms(c, co)
            inner = wall_terms(c, low_half, low_weight, 1.0)
            outer = wall_terms(c, high_half, high_weight, -1.0)
            centre = centre_terms(c, co)
            nxt, prv = theta_terms(c, co)
            above, below = axial_terms(c)
            for k in range(FIELDS):
                inside = jnp.where(is_inner, inner[k], pltpu.roll(to_out[k], 1, 1))
                outside = jnp.where(is_outer, outer[k], pltpu.roll(to_in[k], LANES - 1, 1))
                total = co["inv_r"] * (inside + outside)
                if centre[k] is not None:
                    total = total + centre[k]
                nxt_s[k, pl.ds(b * SUB + SUB, SUB), :] = nxt[k]
                prv_s[k, rows, :] = prv[k]
                swapped_up = pltpu.roll(above[k], HALF, 1)
                swapped_dn = pltpu.roll(below[k], HALF, 1)
                total = total + jnp.where(low, swapped_dn, swapped_up)
                base_ref[a, k, rows, :] = total
                up_s[a, k, rows, :] = swapped_up
                dn_s[a, k, rows, :] = swapped_dn
        for b in range(blocks):
            rows = pl.ds(b * SUB, SUB)
            for k in range(FIELDS):
                base_ref[a, k, rows, :] = (
                    base_ref[a, k, rows, :]
                    + nxt_s[k, pl.ds(b * SUB + SUB - 1, SUB), :]
                    + prv_s[k, pl.ds(b * SUB + 1, SUB), :]
                )
        return carry

    lax.fori_loop(0, pairs, pair, 0)
    old_w, now_w, rate_w = weight_ref[0], weight_ref[1], weight_ref[2]

    def finish(a, carry):
        lower = jnp.maximum(a - 1, 0)
        upper = jnp.minimum(a + 1, pairs - 1)
        has_upper = a < pairs - 1
        first = a == 0
        for b in range(blocks):
            rows = pl.ds(b * SUB, SUB)
            for k in range(FIELDS):
                from_below = up_s[lower, k, rows, :]
                from_below = jnp.where(first, pltpu.roll(from_below, HALF, 1), from_below)
                from_above = jnp.where(has_upper, dn_s[upper, k, rows, :], zero)
                rate = base_ref[a, k, rows, :] + jnp.where(low, from_below, from_above)
                base_ref[a, k, rows, :] = (
                    old_w * old_ref[a, k, rows, :] + now_w * now_ref[a, k, rows, :] + rate_w * rate
                )
        return carry

    lax.fori_loop(0, pairs, finish, 0)


def join_kernel(cycle_cells, flag_ref, weight_ref, base_ref, turn_ref, turn2_ref, inside_ref,
                outside_ref, nxt_ref, prv_ref, state_ref, *sends):
    co = coefficients(flag_ref[0], cycle_cells)
    split, flip, shift = flag_ref[2], flag_ref[3], flag_ref[4]
    rate_w = weight_ref[2]
    lane, place = lanes_of()
    pairs = base_ref.shape[0]
    blocks = base_ref.shape[2] // SUB
    rows_all = blocks * SUB
    row8 = lax.broadcasted_iota(jnp.int32, (SUB, LANES), 0)
    row_id = lax.broadcasted_iota(jnp.int32, (rows_all, LANES), 0)
    from_first = (row_id >= split) != (flip == 1)
    upper_half = lax.broadcasted_iota(jnp.int32, (rows_all, LANES), 1) >= HALF
    weight_r = rate_w * co["inv_r"]
    at_low = jnp.where(place == 0, weight_r, 0.0)
    at_high = jnp.where(place == HALF - 1, weight_r, 0.0)
    at_first = jnp.where(row8 == 0, rate_w, 0.0)
    at_last = jnp.where(row8 == SUB - 1, rate_w, 0.0)

    def opened(value):
        return jnp.concatenate([pltpu.roll(value, HALF, 1), value], axis=0)

    for b in range(blocks):
        rows = pl.ds(b * SUB, SUB)
        inside, outside = inside_ref[rows, :], outside_ref[rows, :]
        for a in range(pairs):
            for k in range(FIELDS):
                j = a * FIELDS + k
                moved = pltpu.roll(inside, LANES - j, 1) if j else inside
                value = base_ref[a, k, rows, :] + at_low * moved
                value = value + at_high * pltpu.roll(outside, HALF - 1 - j, 1)
                if b == 0:
                    value = value + at_first * nxt_ref[j : j + 1, :]
                if b == blocks - 1:
                    value = value + at_last * prv_ref[j : j + 1, :]
                state_ref[a, k, rows, :] = value
    for k in range(FIELDS):
        mixed = jnp.where(from_first, opened(turn_ref[k]), opened(turn2_ref[k]))
        turned = jnp.where(upper_half, pltpu.roll(mixed, shift, 0), 0.0)
        signed = -rate_w if k == 3 else rate_w
        state_ref[pairs - 1, k] = state_ref[pairs - 1, k] + signed * turned
    write_sends(state_ref, co, *sends)


def body(density, velocity, pressure, offsets):
    n_ax, n_az = lax.axis_size("ax"), lax.axis_size("az")
    planes, tile, cells = density.shape[1:]
    cycle_cells = tile * n_az
    is_rotor = lax.axis_index("row") == 0

    vmem = pl.BlockSpec(memory_space=pltpu.VMEM)
    smem = pl.BlockSpec(memory_space=pltpu.SMEM)
    struct = lambda *shape: jax.ShapeDtypeStruct(shape, jnp.float32)
    block = struct(n_ax, FIELDS, tile, LANES)
    edge = struct(n_ax * FIELDS, LANES)
    sends = (struct(FIELDS, tile // 2, LANES), edge, edge, struct(tile, LANES), struct(tile, LANES))

    def device(row, ax, az):
        return (row * n_ax + ax) * n_az + az

    every = [(row, ax, az) for row in range(2) for ax in range(n_ax) for az in range(n_az)]

    def along_az(by):
        return [(device(r, x, z), device(r, x, (z + by) % n_az)) for r, x, z in every]

    def along_ax(by):
        return [
            (device(r, x, z), device(r, x + by, z)) for r, x, z in every if 0 <= x + by < n_ax
        ]

    def turned(by):
        pairs = []
        for x in range(n_ax):
            for z in range(n_az):
                pairs.append((device(1, x, (z + by) % n_az), device(0, x, z)))
                pairs.append((device(0, x, z), device(1, x, (z + by) % n_az)))
        return pairs

    def call(kernel, outs, n_smem, n_vmem, scratch=()):
        return pl.pallas_call(
            kernel,
            out_shape=outs,
            in_specs=[smem] * n_smem + [vmem] * n_vmem,
            out_specs=jax.tree.map(lambda _: vmem, outs),
            scratch_shapes=list(scratch),
            cost_estimate=pl.CostEstimate(
                flops=8_000_000, bytes_accessed=3_000_000, transcendentals=0
            ),
        )

    kernel_of = lambda kernel: functools.partial(kernel, cycle_cells)
    taller = pltpu.VMEM((FIELDS, tile + SUB, LANES), jnp.float32)
    whole = pltpu.VMEM(block.shape, jnp.float32)

    rest = offsets % tile
    segment = jnp.broadcast_to(lax.axis_index("ax"), rest.shape)
    flags = jnp.stack([
        segment,
        jnp.full_like(rest, n_ax),
        jnp.where(is_rotor, rest, tile - rest),
        jnp.where(is_rotor, 0, 1) + jnp.zeros_like(rest),
        jnp.where(is_rotor, (tile - rest) % tile, rest),
    ], axis=1).astype(jnp.int32)
    turns = offsets // tile
    weights = jnp.array([
        [0.0, 1.0, TIME_STEP],
        [0.75, 0.25, 0.25 * TIME_STEP],
        [1.0 / 3.0, 2.0 / 3.0, 2.0 / 3.0 * TIME_STEP],
    ], dtype=jnp.float32)

    chunks = call(pack_kernel, block, 0, 3)(density[0], velocity[0], pressure[0])
    start = lax.all_to_all(chunks, "ax", 0, 0, tiled=True)
    carry = (start, *call(kernel_of(first_kernel), sends, 1, 1)(flags[0], start))

    def local(flag, weight, now):
        return call(kernel_of(local_kernel), block, 2, 2, (taller, taller, whole, whole))(
            flag, weight, start, now
        )

    def around(nxt, prv, out, inn):
        return (
            lax.ppermute(out, AXES, along_ax(1)),
            lax.ppermute(inn, AXES, along_ax(-1)),
            lax.ppermute(nxt, AXES, along_az(1)),
            lax.ppermute(prv, AXES, along_az(-1)),
        )

    def branch(by):
        def run(flag, weight, now, up, *edges):
            ghosts = (
                lax.ppermute(up, AXES, turned(by)),
                lax.ppermute(up, AXES, turned((by + 1) % n_az)),
            )
            if IN_BRANCH:
                ghosts += around(*edges)
                ghosts += (local(flag, weight, now),)
            return ghosts
        return run

    def substep(step, carry):
        now, up, *edges = carry
        flag, weight = flags[step], weights[step]
        if not IN_BRANCH:
            halos = around(*edges)
        ghosts = lax.switch(
            turns[step], [branch(by) for by in range(n_az)], flag, weight, now, up, *edges
        )
        if IN_BRANCH:
            *ghosts, base = ghosts
        else:
            ghosts = (*ghosts, *halos)
            base = local(flag, weight, now)
        return tuple(call(kernel_of(join_kernel), (block, *sends), 2, 7)(
            flag, weight, base, *ghosts
        ))

    if LOOP:
        carry = lax.fori_loop(0, 3, substep, carry)
    else:
        for step in range(3):
            carry = substep(step, carry)
    chunks = lax.all_to_all(carry[0], "ax", 0, 0, tiled=True)
    return call(unpack_kernel, struct(FIELDS, planes, tile, cells), 0, 1)(chunks)[None]


def solution(mesh):
    placed = (
        P("row", "ax", "az", None),
        P("row", None, "ax", "az", None),
        P("row", "ax", "az", None),
        P(),
    )
    return jax.shard_map(
        body,
        mesh=mesh,
        in_specs=placed,
        out_specs=P("row", None, "ax", "az", None),
        check_vma=False,
    )
```

```python
import functools
import math

import jax
import jax.numpy as jnp
from jax import lax
from jax.experimental import pallas as pl
from jax.experimental.pallas import tpu as pltpu
from jax.sharding import PartitionSpec as P

HEAT_RATIO = 1.4
VISCOSITY = 0.8
CONDUCTION = 0.6
TIME_STEP = 0.1
AXIAL_CURVE = 4.0
AXES = ("row", "ax", "az")
FIELDS = 5
SUB = 8
LANES = 128
HALF = 64
EDGE = 4
IN_BRANCH = True
LOOP = True


def cell(state):
    rho, mt, mr, mz, energy = state
    inv = 1.0 / rho
    vt, vr, vz = mt * inv, mr * inv, mz * inv
    tt, rr, zz = mt * vt, mr * vr, mz * vz
    press = (HEAT_RATIO - 1.0) * (energy - 0.5 * (tt + rr + zz))
    visc = (
        None,
        VISCOSITY * vt,
        VISCOSITY * vr,
        VISCOSITY * vz,
        CONDUCTION * (press * inv),
    )
    return dict(
        mt=mt, mr=mr, mz=mz, vt=vt, vr=vr, vz=vz, tt=tt, rr=rr, zz=zz,
        tr=mt * vr, tz=mt * vz, rz=mr * vz, press=press, enth=energy + press, visc=visc,
    )


def flux_theta(c):
    return (c["mt"], c["tt"] + c["press"], c["tr"], c["tz"], c["enth"] * c["vt"])


def flux_radial(c):
    return (c["mr"], c["tr"], c["rr"] + c["press"], c["rz"], c["enth"] * c["vr"])


def flux_axial(c):
    return (c["mz"], c["tz"], c["rz"], c["zz"] + c["press"], c["enth"] * c["vz"])


def axial_terms(c):
    above, below = [], []
    for flux, visc in zip(flux_axial(c), c["visc"]):
        if visc is None:
            above.append(flux)
            below.append(-flux)
        else:
            side = AXIAL_CURVE * visc
            above.append(side + flux)
            below.append(side - flux)
    return above, below


def theta_terms(c, co):
    flux = [co["half_arc"] * f for f in flux_theta(c)]
    flux[1] = flux[1] - co["cross"] * c["visc"][2]
    flux[2] = flux[2] + co["cross"] * c["visc"][1]
    nxt, prv = [flux[0]], [-flux[0]]
    for k in range(1, FIELDS):
        side = co["arc2"] * c["visc"][k]
        nxt.append(side + flux[k])
        prv.append(side - flux[k])
    return nxt, prv


def radial_terms(c, co):
    out, inn = [], []
    for flux, visc in zip(flux_radial(c), c["visc"]):
        odd = co["half_r"] * flux
        if visc is None:
            out.append(odd)
            inn.append(-odd)
        else:
            odd = odd + 0.5 * visc
            even = co["r"] * visc
            out.append(even + odd)
            inn.append(even - odd)
    return out, inn


def wall_terms(c, half_rg, weight, sign):
    flux = flux_radial(c)
    signs = (-1.0, 1.0, 1.0, 1.0, -1.0)
    out = []
    for k in range(FIELDS):
        term = (sign * signs[k]) * (half_rg * flux[k])
        if k:
            term = term + (1.0 if k == 4 else -1.0) * (weight * c["visc"][k])
        out.append(term)
    return out


def centre_terms(c, co):
    centre = [None] + [-(co["centre"] * v) for v in c["visc"][1:]]
    centre[1] = centre[1] - co["inv_r"] * (c["tr"] + co["inv_r"] * c["visc"][1])
    centre[2] = centre[2] + co["inv_r"] * (c["tt"] + c["press"] - co["inv_r"] * c["visc"][2])
    return centre


def lanes_of():
    lane = lax.broadcasted_iota(jnp.int32, (SUB, LANES), 1)
    return lane, jnp.where(lane < HALF, lane, lane - HALF)


def coefficients(segment, cycle_cells):
    dtheta = 2.0 * math.pi / cycle_cells
    cells = (lanes_of()[1] + segment * HALF).astype(jnp.float32)
    r = cycle_cells / (2.0 * math.pi) + cells + 0.5
    inv_r = 1.0 / r
    arc2 = 1.0 / ((r * dtheta) * (r * dtheta))
    return dict(
        r=r, half_r=0.5 * r, inv_r=inv_r, half_arc=1.0 / (2.0 * r * dtheta), arc2=arc2,
        cross=1.0 / (r * r * dtheta), centre=2.0 * arc2 + 2.0 + 2.0 * AXIAL_CURVE,
    )


def pack_kernel(rho_ref, vel_ref, press_ref, out_ref, head_ref, tail_ref):
    lane, _ = lanes_of()
    low = lane < HALF
    first_rows = lax.broadcasted_iota(jnp.int32, (SUB, LANES), 0) < EDGE
    blocks = rho_ref.shape[1] // SUB
    for b in range(blocks):
        rows = pl.ds(b * SUB, SUB)
        for w in range(rho_ref.shape[2] // LANES):
            cols = pl.ds(w * LANES, LANES)
            both = []
            for p in range(2):
                rho = rho_ref[p, rows, cols]
                vel = [vel_ref[d, p, rows, cols] for d in range(3)]
                square = vel[0] * vel[0] + vel[1] * vel[1] + vel[2] * vel[2]
                energy = press_ref[p, rows, cols] / (HEAT_RATIO - 1.0) + 0.5 * rho * square
                both.append([rho] + [rho * v for v in vel] + [energy])
            for k in range(FIELDS):
                first, second = both[0][k], both[1][k]
                inner = jnp.where(low, first, pltpu.roll(second, HALF, 1))
                outer = jnp.where(low, pltpu.roll(first, HALF, 1), second)
                out_ref[2 * w, k, rows, :] = inner
                out_ref[2 * w + 1, k, rows, :] = outer
                if b == 0:
                    head_ref[w, k] = jnp.where(first_rows, inner, pltpu.roll(outer, EDGE, 0))
                if b == blocks - 1:
                    tail_ref[w, k] = jnp.where(first_rows, pltpu.roll(inner, EDGE, 0), outer)


def extend_kernel(in_ref, before_ref, after_ref, out_ref):
    rows = in_ref.shape[2]
    for u in range(in_ref.shape[0]):
        half = pl.ds((u % 2) * EDGE, EDGE)
        for k in range(FIELDS):
            out_ref[u, k, pl.ds(0, EDGE), :] = before_ref[u // 2, k, half, :]
            out_ref[u, k, pl.ds(EDGE, rows), :] = in_ref[u, k]
            out_ref[u, k, pl.ds(EDGE + rows, EDGE), :] = after_ref[u // 2, k, half, :]


def unpack_kernel(in_ref, out_ref):
    lane, _ = lanes_of()
    low = lane < HALF
    for b in range(out_ref.shape[2] // SUB):
        rows = pl.ds(b * SUB, SUB)
        kept = pl.ds(b * SUB + EDGE, SUB)
        for w in range(in_ref.shape[0] // 2):
            cols = pl.ds(w * LANES, LANES)
            for k in range(FIELDS):
                inner, outer = in_ref[2 * w, k, kept, :], in_ref[2 * w + 1, k, kept, :]
                out_ref[k, 0, rows, cols] = jnp.where(low, inner, pltpu.roll(outer, HALF, 1))
                out_ref[k, 1, rows, cols] = jnp.where(low, pltpu.roll(inner, HALF, 1), outer)


def write_sends(state_ref, co, up_ref, out_ref, inn_ref):
    lane, place = lanes_of()
    pairs = state_ref.shape[0]
    blocks = state_ref.shape[2] // SUB
    top = []
    for b in range(blocks):
        rows = pl.ds(b * SUB, SUB)
        packed_out = jnp.zeros((SUB, LANES), jnp.float32)
        packed_in = jnp.zeros((SUB, LANES), jnp.float32)
        for a in range(pairs):
            c = cell([state_ref[a, k, rows, :] for k in range(FIELDS)])
            to_out, to_in = radial_terms(c, co)
            for k in range(FIELDS):
                j = a * FIELDS + k
                here = place == j
                moved = pltpu.roll(to_out[k], (j + 1 - HALF) % LANES, 1)
                packed_out = jnp.where(here, moved, packed_out)
                moved = pltpu.roll(to_in[k], j, 1) if j else to_in[k]
                packed_in = jnp.where(here, moved, packed_in)
            if a == pairs - 1:
                top.append(axial_terms(c)[0])
        out_ref[rows, :] = packed_out
        inn_ref[rows, :] = packed_in
    half = up_ref.shape[1] // SUB
    for b in range(half):
        for k in range(FIELDS):
            value = pltpu.roll(top[b][k], HALF, 1)
            if b + half < blocks:
                value = jnp.where(lane < HALF, value, top[b + half][k])
            up_ref[k, pl.ds(b * SUB, SUB), :] = value


def first_kernel(cycle_cells, flag_ref, state_ref, *sends):
    co = coefficients(flag_ref[0], cycle_cells)
    write_sends(state_ref, co, *sends)


def local_kernel(cycle_cells, flag_ref, weight_ref, old_ref, now_ref, base_ref, nxt_s, prv_s, up_s, dn_s):
    segment, segments = flag_ref[0], flag_ref[1]
    co = coefficients(segment, cycle_cells)
    lane, place = lanes_of()
    low = lane < HALF
    pairs = now_ref.shape[0]
    blocks = now_ref.shape[2] // SUB
    at_inner, at_outer = segment == 0, segment == segments - 1
    is_inner, is_outer = place == 0, place == HALF - 1
    low_half, low_weight = 0.5 * (co["r"] - 1.0), co["r"] - 0.5
    high_half, high_weight = 0.5 * (co["r"] + 1.0), co["r"] + 0.5
    zero = jnp.zeros((SUB, LANES), jnp.float32)
    low_half = jnp.where(at_inner, low_half, zero)
    low_weight = jnp.where(at_inner, low_weight, zero)
    high_half = jnp.where(at_outer, high_half, zero)
    high_weight = jnp.where(at_outer, high_weight, zero)
    rows_end = blocks * SUB
    for k in range(FIELDS):
        nxt_s[k, pl.ds(0, SUB), :] = zero
        prv_s[k, pl.ds(rows_end, SUB), :] = zero

    def pair(a, carry):
        for b in range(blocks):
            rows = pl.ds(b * SUB, SUB)
            c = cell([now_ref[a, k, rows, :] for k in range(FIELDS)])
            to_out, to_in = radial_terms(c, co)
            inner = wall_terms(c, low_half, low_weight, 1.0)
            outer = wall_terms(c, high_half, high_weight, -1.0)
            centre = centre_terms(c, co)
            nxt, prv = theta_terms(c, co)
            above, below = axial_terms(c)
            for k in range(FIELDS):
                inside = jnp.where(is_inner, inner[k], pltpu.roll(to_out[k], 1, 1))
                outside = jnp.where(is_outer, outer[k], pltpu.roll(to_in[k], LANES - 1, 1))
                total = co["inv_r"] * (inside + outside)
                if centre[k] is not None:
                    total = total + centre[k]
                nxt_s[k, pl.ds(b * SUB + SUB, SUB), :] = nxt[k]
                prv_s[k, rows, :] = prv[k]
                swapped_up = pltpu.roll(above[k], HALF, 1)
                swapped_dn = pltpu.roll(below[k], HALF, 1)
                total = total + jnp.where(low, swapped_dn, swapped_up)
                base_ref[a, k, rows, :] = total
                up_s[a, k, rows, :] = swapped_up
                dn_s[a, k, rows, :] = swapped_dn
        for b in range(blocks):
            rows = pl.ds(b * SUB, SUB)
            for k in range(FIELDS):
                base_ref[a, k, rows, :] = (
                    base_ref[a, k, rows, :]
                    + nxt_s[k, pl.ds(b * SUB + SUB - 1, SUB), :]
                    + prv_s[k, pl.ds(b * SUB + 1, SUB), :]
                )
        return carry

    lax.fori_loop(0, pairs, pair, 0)
    old_w, now_w, rate_w = weight_ref[0], weight_ref[1], weight_ref[2]

    def finish(a, carry):
        lower = jnp.maximum(a - 1, 0)
        upper = jnp.minimum(a + 1, pairs - 1)
        has_upper = a < pairs - 1
        first = a == 0
        for b in range(blocks):
            rows = pl.ds(b * SUB, SUB)
            for k in range(FIELDS):
                from_below = up_s[lower, k, rows, :]
                from_below = jnp.where(first, pltpu.roll(from_below, HALF, 1), from_below)
                from_above = jnp.where(has_upper, dn_s[upper, k, rows, :], zero)
                rate = base_ref[a, k, rows, :] + jnp.where(low, from_below, from_above)
                base_ref[a, k, rows, :] = (
                    old_w * old_ref[a, k, rows, :] + now_w * now_ref[a, k, rows, :] + rate_w * rate
                )
        return carry

    lax.fori_loop(0, pairs, finish, 0)


def join_kernel(cycle_cells, flag_ref, weight_ref, base_ref, turn_ref, turn2_ref, inside_ref,
                outside_ref, state_ref, *sends):
    co = coefficients(flag_ref[0], cycle_cells)
    split, flip, shift, shift2 = flag_ref[2], flag_ref[3], flag_ref[4], flag_ref[5]
    rate_w = weight_ref[2]
    lane, place = lanes_of()
    pairs = base_ref.shape[0]
    blocks = base_ref.shape[2] // SUB
    rows_all = blocks * SUB
    row_id = lax.broadcasted_iota(jnp.int32, (rows_all, LANES), 0)
    from_first = (row_id >= split) != (flip == 1)
    upper_half = lax.broadcasted_iota(jnp.int32, (rows_all, LANES), 1) >= HALF
    weight_r = rate_w * co["inv_r"]
    at_low = jnp.where(place == 0, weight_r, 0.0)
    at_high = jnp.where(place == HALF - 1, weight_r, 0.0)

    def opened(value):
        both = jnp.concatenate([pltpu.roll(value, HALF, 1), value], axis=0)
        return both[:rows_all]

    for b in range(blocks):
        rows = pl.ds(b * SUB, SUB)
        inside, outside = inside_ref[rows, :], outside_ref[rows, :]
        for a in range(pairs):
            for k in range(FIELDS):
                j = a * FIELDS + k
                moved = pltpu.roll(inside, LANES - j, 1) if j else inside
                value = base_ref[a, k, rows, :] + at_low * moved
                value = value + at_high * pltpu.roll(outside, HALF - 1 - j, 1)
                state_ref[a, k, rows, :] = value
    for k in range(FIELDS):
        mixed = jnp.where(
            from_first,
            pltpu.roll(opened(turn_ref[k]), shift, 0),
            pltpu.roll(opened(turn2_ref[k]), shift2, 0),
        )
        turned = jnp.where(upper_half, mixed, 0.0)
        signed = -rate_w if k == 3 else rate_w
        state_ref[pairs - 1, k] = state_ref[pairs - 1, k] + signed * turned
    write_sends(state_ref, co, *sends)


def body(density, velocity, pressure, offsets):
    n_ax, n_az = lax.axis_size("ax"), lax.axis_size("az")
    planes, tile, cells = density.shape[1:]
    cycle_cells = tile * n_az
    is_rotor = lax.axis_index("row") == 0

    vmem = pl.BlockSpec(memory_space=pltpu.VMEM)
    smem = pl.BlockSpec(memory_space=pltpu.SMEM)
    struct = lambda *shape: jax.ShapeDtypeStruct(shape, jnp.float32)
    tall = tile + 2 * EDGE
    block = struct(n_ax, FIELDS, tall, LANES)
    outer_rows = struct(n_ax // 2, FIELDS, 2 * EDGE, LANES)
    half_rows = -(-(tall // SUB) // 2) * SUB
    sends = (struct(FIELDS, half_rows, LANES), struct(tall, LANES), struct(tall, LANES))

    def device(row, ax, az):
        return (row * n_ax + ax) * n_az + az

    every = [(row, ax, az) for row in range(2) for ax in range(n_ax) for az in range(n_az)]

    def along_az(by):
        return [(device(r, x, z), device(r, x, (z + by) % n_az)) for r, x, z in every]

    def along_ax(by):
        return [
            (device(r, x, z), device(r, x + by, z)) for r, x, z in every if 0 <= x + by < n_ax
        ]

    def turned(by):
        pairs = []
        for x in range(n_ax):
            for z in range(n_az):
                pairs.append((device(1, x, (z + by) % n_az), device(0, x, z)))
                pairs.append((device(0, x, z), device(1, x, (z + by) % n_az)))
        return pairs

    def call(kernel, outs, n_smem, n_vmem, scratch=()):
        return pl.pallas_call(
            kernel,
            out_shape=outs,
            in_specs=[smem] * n_smem + [vmem] * n_vmem,
            out_specs=jax.tree.map(lambda _: vmem, outs),
            scratch_shapes=list(scratch),
            cost_estimate=pl.CostEstimate(
                flops=8_000_000, bytes_accessed=3_000_000, transcendentals=0
            ),
        )

    kernel_of = lambda kernel: functools.partial(kernel, cycle_cells)
    taller = pltpu.VMEM((FIELDS, tall + SUB, LANES), jnp.float32)
    whole = pltpu.VMEM(block.shape, jnp.float32)

    chunks, head, tail = call(
        pack_kernel, (struct(n_ax, FIELDS, tile, LANES), outer_rows, outer_rows), 0, 3
    )(density[0], velocity[0], pressure[0])
    before = lax.ppermute(tail, AXES, along_az(1))
    after = lax.ppermute(head, AXES, along_az(-1))
    chunks = call(extend_kernel, block, 0, 3)(chunks, before, after)
    start = lax.all_to_all(chunks, "ax", 0, 0, tiled=True)

    segment = lax.axis_index("ax")
    flags, turns, weights = [], [], []
    for step, (old_w, now_w) in enumerate(((0.0, 1.0), (0.75, 0.25), (1.0 / 3.0, 2.0 / 3.0))):
        rest = offsets[step] % tile
        turns.append(offsets[step] // tile)
        flags.append(jnp.stack([
            segment,
            jnp.full_like(segment, n_ax),
            jnp.where(is_rotor, tile + EDGE - rest, EDGE + rest),
            jnp.where(is_rotor, 1, 0),
            jnp.where(is_rotor, (tall - rest) % tall, rest),
            jnp.where(is_rotor, tile - rest, rest + tall - tile),
        ]).astype(jnp.int32))
        weights.append(jnp.array([old_w, now_w, now_w * TIME_STEP], dtype=jnp.float32))
    carry = (start, *call(kernel_of(first_kernel), sends, 1, 1)(flags[0], start))

    def local(flag, weight, now):
        return call(kernel_of(local_kernel), block, 2, 2, (taller, taller, whole, whole))(
            flag, weight, start, now
        )

    def around(out, inn):
        return (
            lax.ppermute(out, AXES, along_ax(1)),
            lax.ppermute(inn, AXES, along_ax(-1)),
        )

    def branch(by):
        def run(flag, weight, now, up, *edges):
            ghosts = (
                lax.ppermute(up, AXES, turned(by)),
                lax.ppermute(up, AXES, turned((by + 1) % n_az)),
            )
            if IN_BRANCH:
                ghosts += around(*edges)
                ghosts += (local(flag, weight, now),)
            return ghosts
        return run

    def substep(_, carry):
        now, up, *edges = carry[:4]
        turns, flags, weights = carry[4:]
        flag, weight = flags[0], weights[0]
        if not IN_BRANCH:
            halos = around(*edges)
        ghosts = lax.switch(
            turns[0], [branch(by) for by in range(n_az)], flag, weight, now, up, *edges
        )
        if IN_BRANCH:
            *ghosts, base = ghosts
        else:
            ghosts = (*ghosts, *halos)
            base = local(flag, weight, now)
        state = call(kernel_of(join_kernel), (block, *sends), 2, 5)(flag, weight, base, *ghosts)
        later = lambda kept: (*kept[1:], kept[0])
        return (*state, later(turns), later(flags), later(weights))

    carry = (*carry, tuple(turns), tuple(flags), tuple(weights))
    if LOOP:
        carry = lax.fori_loop(0, 3, substep, carry)
    else:
        for step in range(3):
            carry = substep(step, carry)
    chunks = lax.all_to_all(carry[0], "ax", 0, 0, tiled=True)
    return call(unpack_kernel, struct(FIELDS, planes, tile, cells), 0, 1)(chunks)[None]


def solution(mesh):
    placed = (
        P("row", "ax", "az", None),
        P("row", None, "ax", "az", None),
        P("row", "ax", "az", None),
        P(),
    )
    return jax.shard_map(
        body,
        mesh=mesh,
        in_specs=placed,
        out_specs=P("row", None, "ax", "az", None),
        check_vma=False,
    )
```

```python
import functools
import math

import jax
import jax.numpy as jnp
from jax import lax
from jax.experimental import pallas as pl
from jax.experimental.pallas import tpu as pltpu
from jax.sharding import PartitionSpec as P

HEAT_RATIO = 1.4
VISCOSITY = 0.8
CONDUCTION = 0.6
TIME_STEP = 0.1
AXIAL_CURVE = 4.0
AXES = ("row", "ax", "az")
FIELDS = 5
SUB = 8
LANES = 128
HALF = 64
EDGE = 4
IN_BRANCH = True
LOOP = True


def cell(state):
    rho, mt, mr, mz, energy = state
    inv = 1.0 / rho
    vt, vr, vz = mt * inv, mr * inv, mz * inv
    tt, rr, zz = mt * vt, mr * vr, mz * vz
    press = (HEAT_RATIO - 1.0) * (energy - 0.5 * (tt + rr + zz))
    visc = (
        None,
        VISCOSITY * vt,
        VISCOSITY * vr,
        VISCOSITY * vz,
        CONDUCTION * (press * inv),
    )
    return dict(
        mt=mt, mr=mr, mz=mz, vt=vt, vr=vr, vz=vz, tt=tt, rr=rr, zz=zz,
        tr=mt * vr, tz=mt * vz, rz=mr * vz, press=press, enth=energy + press, visc=visc,
    )


def flux_theta(c):
    return (c["mt"], c["tt"] + c["press"], c["tr"], c["tz"], c["enth"] * c["vt"])


def flux_radial(c):
    return (c["mr"], c["tr"], c["rr"] + c["press"], c["rz"], c["enth"] * c["vr"])


def flux_axial(c):
    return (c["mz"], c["tz"], c["rz"], c["zz"] + c["press"], c["enth"] * c["vz"])


def axial_terms(c):
    above, below = [], []
    for flux, visc in zip(flux_axial(c), c["visc"]):
        if visc is None:
            above.append(flux)
            below.append(-flux)
        else:
            side = AXIAL_CURVE * visc
            above.append(side + flux)
            below.append(side - flux)
    return above, below


def theta_terms(c, co):
    flux = [co["half_arc"] * f for f in flux_theta(c)]
    flux[1] = flux[1] - co["cross"] * c["visc"][2]
    flux[2] = flux[2] + co["cross"] * c["visc"][1]
    nxt, prv = [flux[0]], [-flux[0]]
    for k in range(1, FIELDS):
        side = co["arc2"] * c["visc"][k]
        nxt.append(side + flux[k])
        prv.append(side - flux[k])
    return nxt, prv


def radial_terms(c, co):
    out, inn = [], []
    for flux, visc in zip(flux_radial(c), c["visc"]):
        odd = co["half_r"] * flux
        if visc is None:
            out.append(odd)
            inn.append(-odd)
        else:
            odd = odd + 0.5 * visc
            even = co["r"] * visc
            out.append(even + odd)
            inn.append(even - odd)
    return out, inn


def wall_terms(c, half_rg, weight, sign):
    flux = flux_radial(c)
    signs = (-1.0, 1.0, 1.0, 1.0, -1.0)
    out = []
    for k in range(FIELDS):
        term = (sign * signs[k]) * (half_rg * flux[k])
        if k:
            term = term + (1.0 if k == 4 else -1.0) * (weight * c["visc"][k])
        out.append(term)
    return out


def centre_terms(c, co):
    centre = [None] + [-(co["centre"] * v) for v in c["visc"][1:]]
    centre[1] = centre[1] - co["inv_r"] * (c["tr"] + co["inv_r"] * c["visc"][1])
    centre[2] = centre[2] + co["inv_r"] * (c["tt"] + c["press"] - co["inv_r"] * c["visc"][2])
    return centre


def lanes_of():
    lane = lax.broadcasted_iota(jnp.int32, (SUB, LANES), 1)
    return lane, jnp.where(lane < HALF, lane, lane - HALF)


def coefficients(segment, cycle_cells):
    dtheta = 2.0 * math.pi / cycle_cells
    cells = (lanes_of()[1] + segment * HALF).astype(jnp.float32)
    r = cycle_cells / (2.0 * math.pi) + cells + 0.5
    inv_r = 1.0 / r
    arc2 = 1.0 / ((r * dtheta) * (r * dtheta))
    return dict(
        r=r, half_r=0.5 * r, inv_r=inv_r, half_arc=1.0 / (2.0 * r * dtheta), arc2=arc2,
        cross=1.0 / (r * r * dtheta), centre=2.0 * arc2 + 2.0 + 2.0 * AXIAL_CURVE,
    )


def pack_kernel(rho_ref, vel_ref, press_ref, out_ref):
    lane, _ = lanes_of()
    low = lane < HALF
    for b in range(rho_ref.shape[1] // SUB):
        rows = pl.ds(b * SUB, SUB)
        for w in range(rho_ref.shape[2] // LANES):
            cols = pl.ds(w * LANES, LANES)
            both = []
            for p in range(2):
                rho = rho_ref[p, rows, cols]
                vel = [vel_ref[d, p, rows, cols] for d in range(3)]
                square = vel[0] * vel[0] + vel[1] * vel[1] + vel[2] * vel[2]
                energy = press_ref[p, rows, cols] / (HEAT_RATIO - 1.0) + 0.5 * rho * square
                both.append([rho] + [rho * v for v in vel] + [energy])
            for k in range(FIELDS):
                first, second = both[0][k], both[1][k]
                out_ref[2 * w, k, rows, :] = jnp.where(low, first, pltpu.roll(second, HALF, 1))
                out_ref[2 * w + 1, k, rows, :] = jnp.where(low, pltpu.roll(first, HALF, 1), second)


def edge_kernel(flag_ref, in_ref, up_ref, down_ref):
    front = lax.broadcasted_iota(jnp.int32, (SUB, LANES), 0) < EDGE
    rotor = flag_ref[6] == 1
    end = pl.ds(in_ref.shape[2] - SUB, SUB)
    for i in range(up_ref.shape[0]):
        one, two = divmod(2 * i, FIELDS), divmod(2 * i + 1, FIELDS)
        head = jnp.where(
            front, in_ref[*one, pl.ds(0, SUB), :], pltpu.roll(in_ref[*two, pl.ds(0, SUB), :], EDGE, 0)
        )
        tail = jnp.where(front, pltpu.roll(in_ref[*one, end, :], EDGE, 0), in_ref[*two, end, :])
        up_ref[i] = jnp.where(rotor, tail, head)
        down_ref[i] = jnp.where(rotor, head, tail)


def unpack_kernel(in_ref, out_ref):
    lane, _ = lanes_of()
    low = lane < HALF
    for b in range(out_ref.shape[2] // SUB):
        rows = pl.ds(b * SUB, SUB)
        for w in range(in_ref.shape[0] // 2):
            cols = pl.ds(w * LANES, LANES)
            for k in range(FIELDS):
                inner, outer = in_ref[2 * w, k, rows, :], in_ref[2 * w + 1, k, rows, :]
                out_ref[k, 0, rows, cols] = jnp.where(low, inner, pltpu.roll(outer, HALF, 1))
                out_ref[k, 1, rows, cols] = jnp.where(low, pltpu.roll(inner, HALF, 1), outer)


def write_sends(state_ref, co, up_ref, out_ref, inn_ref):
    lane, place = lanes_of()
    pairs = state_ref.shape[0]
    blocks = state_ref.shape[2] // SUB
    top = []
    for b in range(blocks):
        rows = pl.ds(b * SUB, SUB)
        packed_out = jnp.zeros((SUB, LANES), jnp.float32)
        packed_in = jnp.zeros((SUB, LANES), jnp.float32)
        for a in range(pairs):
            c = cell([state_ref[a, k, rows, :] for k in range(FIELDS)])
            to_out, to_in = radial_terms(c, co)
            for k in range(FIELDS):
                j = a * FIELDS + k
                here = place == j
                moved = pltpu.roll(to_out[k], (j + 1 - HALF) % LANES, 1)
                packed_out = jnp.where(here, moved, packed_out)
                moved = pltpu.roll(to_in[k], j, 1) if j else to_in[k]
                packed_in = jnp.where(here, moved, packed_in)
            if a == pairs - 1:
                top.append(axial_terms(c)[0])
        out_ref[rows, :] = packed_out
        inn_ref[rows, :] = packed_in
    half = up_ref.shape[1] // SUB
    for b in range(half):
        for k in range(FIELDS):
            value = pltpu.roll(top[b][k], HALF, 1)
            if b + half < blocks:
                value = jnp.where(lane < HALF, value, top[b + half][k])
            up_ref[k, pl.ds(b * SUB, SUB), :] = value


def first_kernel(cycle_cells, flag_ref, in_ref, one_ref, two_ref, state_ref, *sends):
    rotor = flag_ref[6] == 1
    rows = in_ref.shape[2]
    for a in range(in_ref.shape[0]):
        for k in range(FIELDS):
            i, half = divmod(a * FIELDS + k, 2)
            half = pl.ds(half * EDGE, EDGE)
            one, two = one_ref[i, half, :], two_ref[i, half, :]
            state_ref[a, k, pl.ds(0, EDGE), :] = jnp.where(rotor, one, two)
            state_ref[a, k, pl.ds(EDGE, rows), :] = in_ref[a, k]
            state_ref[a, k, pl.ds(EDGE + rows, EDGE), :] = jnp.where(rotor, two, one)
    co = coefficients(flag_ref[0], cycle_cells)
    write_sends(state_ref, co, *sends)


def local_kernel(cycle_cells, flag_ref, weight_ref, old_ref, now_ref, base_ref, nxt_s, prv_s, up_s, dn_s):
    segment, segments = flag_ref[0], flag_ref[1]
    co = coefficients(segment, cycle_cells)
    lane, place = lanes_of()
    low = lane < HALF
    pairs = now_ref.shape[0]
    blocks = now_ref.shape[2] // SUB
    at_inner, at_outer = segment == 0, segment == segments - 1
    is_inner, is_outer = place == 0, place == HALF - 1
    low_half, low_weight = 0.5 * (co["r"] - 1.0), co["r"] - 0.5
    high_half, high_weight = 0.5 * (co["r"] + 1.0), co["r"] + 0.5
    zero = jnp.zeros((SUB, LANES), jnp.float32)
    low_half = jnp.where(at_inner, low_half, zero)
    low_weight = jnp.where(at_inner, low_weight, zero)
    high_half = jnp.where(at_outer, high_half, zero)
    high_weight = jnp.where(at_outer, high_weight, zero)
    rows_end = blocks * SUB
    for k in range(FIELDS):
        nxt_s[k, pl.ds(0, SUB), :] = zero
        prv_s[k, pl.ds(rows_end, SUB), :] = zero

    def pair(a, carry):
        for b in range(blocks):
            rows = pl.ds(b * SUB, SUB)
            c = cell([now_ref[a, k, rows, :] for k in range(FIELDS)])
            to_out, to_in = radial_terms(c, co)
            inner = wall_terms(c, low_half, low_weight, 1.0)
            outer = wall_terms(c, high_half, high_weight, -1.0)
            centre = centre_terms(c, co)
            nxt, prv = theta_terms(c, co)
            above, below = axial_terms(c)
            for k in range(FIELDS):
                inside = jnp.where(is_inner, inner[k], pltpu.roll(to_out[k], 1, 1))
                outside = jnp.where(is_outer, outer[k], pltpu.roll(to_in[k], LANES - 1, 1))
                total = co["inv_r"] * (inside + outside)
                if centre[k] is not None:
                    total = total + centre[k]
                nxt_s[k, pl.ds(b * SUB + SUB, SUB), :] = nxt[k]
                prv_s[k, rows, :] = prv[k]
                swapped_up = pltpu.roll(above[k], HALF, 1)
                swapped_dn = pltpu.roll(below[k], HALF, 1)
                total = total + jnp.where(low, swapped_dn, swapped_up)
                base_ref[a, k, rows, :] = total
                up_s[a, k, rows, :] = swapped_up
                dn_s[a, k, rows, :] = swapped_dn
        for b in range(blocks):
            rows = pl.ds(b * SUB, SUB)
            for k in range(FIELDS):
                base_ref[a, k, rows, :] = (
                    base_ref[a, k, rows, :]
                    + nxt_s[k, pl.ds(b * SUB + SUB - 1, SUB), :]
                    + prv_s[k, pl.ds(b * SUB + 1, SUB), :]
                )
        return carry

    lax.fori_loop(0, pairs, pair, 0)
    old_w, now_w, rate_w = weight_ref[0], weight_ref[1], weight_ref[2]

    def finish(a, carry):
        lower = jnp.maximum(a - 1, 0)
        upper = jnp.minimum(a + 1, pairs - 1)
        has_upper = a < pairs - 1
        first = a == 0
        for b in range(blocks):
            rows = pl.ds(b * SUB, SUB)
            for k in range(FIELDS):
                from_below = up_s[lower, k, rows, :]
                from_below = jnp.where(first, pltpu.roll(from_below, HALF, 1), from_below)
                from_above = jnp.where(has_upper, dn_s[upper, k, rows, :], zero)
                rate = base_ref[a, k, rows, :] + jnp.where(low, from_below, from_above)
                base_ref[a, k, rows, :] = (
                    old_w * old_ref[a, k, rows, :] + now_w * now_ref[a, k, rows, :] + rate_w * rate
                )
        return carry

    lax.fori_loop(0, pairs, finish, 0)


def join_kernel(cycle_cells, flag_ref, weight_ref, base_ref, turn_ref, turn2_ref, inside_ref,
                outside_ref, state_ref, own_ref, *sends):
    co = coefficients(flag_ref[0], cycle_cells)
    split, flip, shift, shift2 = flag_ref[2], flag_ref[3], flag_ref[4], flag_ref[5]
    rate_w = weight_ref[2]
    lane, place = lanes_of()
    pairs = base_ref.shape[0]
    blocks = base_ref.shape[2] // SUB
    rows_all = blocks * SUB
    row_id = lax.broadcasted_iota(jnp.int32, (rows_all, LANES), 0)
    from_first = (row_id >= split) != (flip == 1)
    upper_half = lax.broadcasted_iota(jnp.int32, (rows_all, LANES), 1) >= HALF
    weight_r = rate_w * co["inv_r"]
    at_low = jnp.where(place == 0, weight_r, 0.0)
    at_high = jnp.where(place == HALF - 1, weight_r, 0.0)

    def opened(value):
        both = jnp.concatenate([pltpu.roll(value, HALF, 1), value], axis=0)
        return both[:rows_all]

    for b in range(blocks):
        rows = pl.ds(b * SUB, SUB)
        inside, outside = inside_ref[rows, :], outside_ref[rows, :]
        for a in range(pairs):
            for k in range(FIELDS):
                j = a * FIELDS + k
                moved = pltpu.roll(inside, LANES - j, 1) if j else inside
                value = base_ref[a, k, rows, :] + at_low * moved
                value = value + at_high * pltpu.roll(outside, HALF - 1 - j, 1)
                state_ref[a, k, rows, :] = value
    for k in range(FIELDS):
        mixed = jnp.where(
            from_first,
            pltpu.roll(opened(turn_ref[k]), shift, 0),
            pltpu.roll(opened(turn2_ref[k]), shift2, 0),
        )
        turned = jnp.where(upper_half, mixed, 0.0)
        signed = -rate_w if k == 3 else rate_w
        state_ref[pairs - 1, k] = state_ref[pairs - 1, k] + signed * turned
    for a in range(pairs):
        for k in range(FIELDS):
            own_ref[a, k] = state_ref[a, k, pl.ds(EDGE, own_ref.shape[2]), :]
    write_sends(state_ref, co, *sends)


def body(density, velocity, pressure, offsets):
    n_ax, n_az = lax.axis_size("ax"), lax.axis_size("az")
    planes, tile, cells = density.shape[1:]
    cycle_cells = tile * n_az
    is_rotor = lax.axis_index("row") == 0

    vmem = pl.BlockSpec(memory_space=pltpu.VMEM)
    smem = pl.BlockSpec(memory_space=pltpu.SMEM)
    struct = lambda *shape: jax.ShapeDtypeStruct(shape, jnp.float32)
    tall = tile + 2 * EDGE
    block = struct(n_ax, FIELDS, tall, LANES)
    own = struct(n_ax, FIELDS, tile, LANES)
    outer_rows = struct(n_ax * FIELDS // 2, 2 * EDGE, LANES)
    half_rows = -(-(tall // SUB) // 2) * SUB
    sends = (struct(FIELDS, half_rows, LANES), struct(tall, LANES), struct(tall, LANES))

    def device(row, ax, az):
        return (row * n_ax + ax) * n_az + az

    every = [(row, ax, az) for row in range(2) for ax in range(n_ax) for az in range(n_az)]

    def along_ax(by):
        return [
            (device(r, x, z), device(r, x + by, z)) for r, x, z in every if 0 <= x + by < n_ax
        ]

    def turned(by):
        pairs = []
        for x in range(n_ax):
            for z in range(n_az):
                pairs.append((device(1, x, (z + by) % n_az), device(0, x, z)))
                pairs.append((device(0, x, z), device(1, x, (z + by) % n_az)))
        return pairs

    def call(kernel, outs, n_smem, n_vmem, scratch=()):
        return pl.pallas_call(
            kernel,
            out_shape=outs,
            in_specs=[smem] * n_smem + [vmem] * n_vmem,
            out_specs=jax.tree.map(lambda _: vmem, outs),
            scratch_shapes=list(scratch),
            cost_estimate=pl.CostEstimate(
                flops=8_000_000, bytes_accessed=3_000_000, transcendentals=0
            ),
        )

    kernel_of = lambda kernel: functools.partial(kernel, cycle_cells)
    taller = pltpu.VMEM((FIELDS, tall + SUB, LANES), jnp.float32)
    whole = pltpu.VMEM(block.shape, jnp.float32)

    chunks = call(pack_kernel, own, 0, 3)(density[0], velocity[0], pressure[0])
    whole_tile = lax.all_to_all(chunks, "ax", 0, 0, tiled=True)

    segment = lax.axis_index("ax")
    flags, turns, weights = [], [], []
    for step, (old_w, now_w) in enumerate(((0.0, 1.0), (0.75, 0.25), (1.0 / 3.0, 2.0 / 3.0))):
        rest = offsets[step] % tile
        turns.append(offsets[step] // tile)
        flags.append(jnp.stack([
            segment,
            jnp.full_like(segment, n_ax),
            jnp.where(is_rotor, tile + EDGE - rest, EDGE + rest),
            jnp.where(is_rotor, 1, 0),
            jnp.where(is_rotor, (tall - rest) % tall, rest),
            jnp.where(is_rotor, tile - rest, rest + tall - tile),
            jnp.where(is_rotor, 1, 0),
        ]).astype(jnp.int32))
        weights.append(jnp.array([old_w, now_w, now_w * TIME_STEP], dtype=jnp.float32))
    up_rows, down_rows = call(edge_kernel, (outer_rows, outer_rows), 1, 1)(flags[0], whole_tile)
    up_rows = lax.ppermute(up_rows, AXES, turned(1))
    down_rows = lax.ppermute(down_rows, AXES, turned(n_az - 1))
    up_rows = lax.ppermute(up_rows, AXES, turned(0))
    down_rows = lax.ppermute(down_rows, AXES, turned(0))
    start, *first = call(kernel_of(first_kernel), (block, *sends), 1, 3)(
        flags[0], whole_tile, up_rows, down_rows
    )
    carry = (start, whole_tile, *first)

    def local(flag, weight, now):
        return call(kernel_of(local_kernel), block, 2, 2, (taller, taller, whole, whole))(
            flag, weight, start, now
        )

    def around(out, inn):
        return (
            lax.ppermute(out, AXES, along_ax(1)),
            lax.ppermute(inn, AXES, along_ax(-1)),
        )

    def branch(by):
        def run(flag, weight, now, up, *edges):
            ghosts = (
                lax.ppermute(up, AXES, turned(by)),
                lax.ppermute(up, AXES, turned((by + 1) % n_az)),
            )
            if IN_BRANCH:
                ghosts += around(*edges)
                ghosts += (local(flag, weight, now),)
            return ghosts
        return run

    def substep(_, carry):
        now, _, up, *edges = carry[:5]
        turns, flags, weights = carry[5:]
        flag, weight = flags[0], weights[0]
        if not IN_BRANCH:
            halos = around(*edges)
        ghosts = lax.switch(
            turns[0], [branch(by) for by in range(n_az)], flag, weight, now, up, *edges
        )
        if IN_BRANCH:
            *ghosts, base = ghosts
        else:
            ghosts = (*ghosts, *halos)
            base = local(flag, weight, now)
        state = call(kernel_of(join_kernel), (block, own, *sends), 2, 5)(
            flag, weight, base, *ghosts
        )
        later = lambda kept: (*kept[1:], kept[0])
        return (*state, later(turns), later(flags), later(weights))

    carry = (*carry, tuple(turns), tuple(flags), tuple(weights))
    if LOOP:
        carry = lax.fori_loop(0, 3, substep, carry)
    else:
        for step in range(3):
            carry = substep(step, carry)
    chunks = lax.all_to_all(carry[1], "ax", 0, 0, tiled=True)
    return call(unpack_kernel, struct(FIELDS, planes, tile, cells), 0, 1)(chunks)[None]


def solution(mesh):
    placed = (
        P("row", "ax", "az", None),
        P("row", None, "ax", "az", None),
        P("row", "ax", "az", None),
        P(),
    )
    return jax.shard_map(
        body,
        mesh=mesh,
        in_specs=placed,
        out_specs=P("row", None, "ax", "az", None),
        check_vma=False,
    )
```

```python
import functools
import math

import jax
import jax.numpy as jnp
from jax import lax
from jax.experimental import pallas as pl
from jax.experimental.pallas import tpu as pltpu
from jax.sharding import PartitionSpec as P

HEAT_RATIO = 1.4
VISCOSITY = 0.8
CONDUCTION = 0.6
TIME_STEP = 0.1
AXIAL_CURVE = 4.0
AXES = ("row", "ax", "az")
FIELDS = 5
SUB = 8
LANES = 128
HALF = 64
EDGE = 4


def cell(state):
    rho, mt, mr, mz, energy = state
    inv = 1.0 / rho
    vt, vr, vz = mt * inv, mr * inv, mz * inv
    tt, rr, zz = mt * vt, mr * vr, mz * vz
    press = (HEAT_RATIO - 1.0) * (energy - 0.5 * (tt + rr + zz))
    visc = (
        None,
        VISCOSITY * vt,
        VISCOSITY * vr,
        VISCOSITY * vz,
        CONDUCTION * (press * inv),
    )
    return dict(
        mt=mt, mr=mr, mz=mz, vt=vt, vr=vr, vz=vz, tt=tt, rr=rr, zz=zz,
        tr=mt * vr, tz=mt * vz, rz=mr * vz, press=press, enth=energy + press, visc=visc,
    )


def flux_theta(c):
    return (c["mt"], c["tt"] + c["press"], c["tr"], c["tz"], c["enth"] * c["vt"])


def flux_radial(c):
    return (c["mr"], c["tr"], c["rr"] + c["press"], c["rz"], c["enth"] * c["vr"])


def flux_axial(c):
    return (c["mz"], c["tz"], c["rz"], c["zz"] + c["press"], c["enth"] * c["vz"])


def axial_terms(c):
    above, below = [], []
    for flux, visc in zip(flux_axial(c), c["visc"]):
        if visc is None:
            above.append(flux)
            below.append(-flux)
        else:
            side = AXIAL_CURVE * visc
            above.append(side + flux)
            below.append(side - flux)
    return above, below


def theta_terms(c, co):
    flux = [co["half_arc"] * f for f in flux_theta(c)]
    flux[1] = flux[1] - co["cross"] * c["visc"][2]
    flux[2] = flux[2] + co["cross"] * c["visc"][1]
    nxt, prv = [flux[0]], [-flux[0]]
    for k in range(1, FIELDS):
        side = co["arc2"] * c["visc"][k]
        nxt.append(side + flux[k])
        prv.append(side - flux[k])
    return nxt, prv


def radial_terms(c, co):
    out, inn = [], []
    for flux, visc in zip(flux_radial(c), c["visc"]):
        odd = co["half_r"] * flux
        if visc is None:
            out.append(odd)
            inn.append(-odd)
        else:
            odd = odd + 0.5 * visc
            even = co["r"] * visc
            out.append(even + odd)
            inn.append(even - odd)
    return out, inn


def wall_terms(c, half_rg, weight, sign):
    flux = flux_radial(c)
    signs = (-1.0, 1.0, 1.0, 1.0, -1.0)
    out = []
    for k in range(FIELDS):
        term = (sign * signs[k]) * (half_rg * flux[k])
        if k:
            term = term + (1.0 if k == 4 else -1.0) * (weight * c["visc"][k])
        out.append(term)
    return out


def centre_terms(c, co):
    centre = [None] + [-(co["centre"] * v) for v in c["visc"][1:]]
    centre[1] = centre[1] - co["inv_r"] * (c["tr"] + co["inv_r"] * c["visc"][1])
    centre[2] = centre[2] + co["inv_r"] * (c["tt"] + c["press"] - co["inv_r"] * c["visc"][2])
    return centre


def lanes_of():
    lane = lax.broadcasted_iota(jnp.int32, (SUB, LANES), 1)
    return lane, jnp.where(lane < HALF, lane, lane - HALF)


def coefficients(segment, cycle_cells):
    dtheta = 2.0 * math.pi / cycle_cells
    cells = (lanes_of()[1] + segment * HALF).astype(jnp.float32)
    r = cycle_cells / (2.0 * math.pi) + cells + 0.5
    inv_r = 1.0 / r
    arc2 = 1.0 / ((r * dtheta) * (r * dtheta))
    return dict(
        r=r, half_r=0.5 * r, inv_r=inv_r, half_arc=1.0 / (2.0 * r * dtheta), arc2=arc2,
        cross=1.0 / (r * r * dtheta), centre=2.0 * arc2 + 2.0 + 2.0 * AXIAL_CURVE,
    )


def weights_of(step):
    first, second = step == 0, step == 1
    old = jnp.where(first, 0.0, jnp.where(second, 0.75, 1.0 / 3.0))
    now = jnp.where(first, 1.0, jnp.where(second, 0.25, 2.0 / 3.0))
    return old, now, now * TIME_STEP


def decode(code_ref, segments):
    code = code_ref[0]
    place = lax.div(code, 4)
    return lax.rem(code, 4), lax.rem(place, segments), lax.div(place, segments) == 1


def pack_kernel(rho_ref, vel_ref, press_ref, out_ref):
    lane, _ = lanes_of()
    low = lane < HALF
    for b in range(rho_ref.shape[1] // SUB):
        rows = pl.ds(b * SUB, SUB)
        for w in range(rho_ref.shape[2] // LANES):
            cols = pl.ds(w * LANES, LANES)
            both = []
            for p in range(2):
                rho = rho_ref[p, rows, cols]
                vel = [vel_ref[d, p, rows, cols] for d in range(3)]
                square = vel[0] * vel[0] + vel[1] * vel[1] + vel[2] * vel[2]
                energy = press_ref[p, rows, cols] / (HEAT_RATIO - 1.0) + 0.5 * rho * square
                both.append([rho] + [rho * v for v in vel] + [energy])
            for k in range(FIELDS):
                first, second = both[0][k], both[1][k]
                out_ref[2 * w, k, rows, :] = jnp.where(low, first, pltpu.roll(second, HALF, 1))
                out_ref[2 * w + 1, k, rows, :] = jnp.where(low, pltpu.roll(first, HALF, 1), second)


def edge_kernel(code_ref, in_ref, up_ref, down_ref):
    front = lax.broadcasted_iota(jnp.int32, (SUB, LANES), 0) < EDGE
    _, _, rotor = decode(code_ref, in_ref.shape[0])
    end = pl.ds(in_ref.shape[2] - SUB, SUB)
    for i in range(up_ref.shape[0]):
        one, two = divmod(2 * i, FIELDS), divmod(2 * i + 1, FIELDS)
        head = jnp.where(
            front, in_ref[*one, pl.ds(0, SUB), :], pltpu.roll(in_ref[*two, pl.ds(0, SUB), :], EDGE, 0)
        )
        tail = jnp.where(front, pltpu.roll(in_ref[*one, end, :], EDGE, 0), in_ref[*two, end, :])
        up_ref[i] = jnp.where(rotor, tail, head)
        down_ref[i] = jnp.where(rotor, head, tail)


def unpack_kernel(in_ref, out_ref):
    lane, _ = lanes_of()
    low = lane < HALF
    for b in range(out_ref.shape[2] // SUB):
        rows = pl.ds(b * SUB, SUB)
        for w in range(in_ref.shape[0] // 2):
            cols = pl.ds(w * LANES, LANES)
            for k in range(FIELDS):
                inner, outer = in_ref[2 * w, k, rows, :], in_ref[2 * w + 1, k, rows, :]
                out_ref[k, 0, rows, cols] = jnp.where(low, inner, pltpu.roll(outer, HALF, 1))
                out_ref[k, 1, rows, cols] = jnp.where(low, pltpu.roll(inner, HALF, 1), outer)


def write_sends(state_ref, co, up_ref, out_ref, inn_ref):
    lane, place = lanes_of()
    pairs = state_ref.shape[0]
    blocks = state_ref.shape[2] // SUB
    top = []
    for b in range(blocks):
        rows = pl.ds(b * SUB, SUB)
        packed_out = jnp.zeros((SUB, LANES), jnp.float32)
        packed_in = jnp.zeros((SUB, LANES), jnp.float32)
        for a in range(pairs):
            c = cell([state_ref[a, k, rows, :] for k in range(FIELDS)])
            to_out, to_in = radial_terms(c, co)
            for k in range(FIELDS):
                j = a * FIELDS + k
                here = place == j
                moved = pltpu.roll(to_out[k], (j + 1 - HALF) % LANES, 1)
                packed_out = jnp.where(here, moved, packed_out)
                moved = pltpu.roll(to_in[k], j, 1) if j else to_in[k]
                packed_in = jnp.where(here, moved, packed_in)
            if a == pairs - 1:
                top.append(axial_terms(c)[0])
        out_ref[rows, :] = packed_out
        inn_ref[rows, :] = packed_in
    half = up_ref.shape[1] // SUB
    for b in range(half):
        for k in range(FIELDS):
            value = pltpu.roll(top[b][k], HALF, 1)
            if b + half < blocks:
                value = jnp.where(lane < HALF, value, top[b + half][k])
            up_ref[k, pl.ds(b * SUB, SUB), :] = value


def first_kernel(cycle_cells, code_ref, in_ref, one_ref, two_ref, state_ref, *sends):
    _, segment, rotor = decode(code_ref, in_ref.shape[0])
    rows = in_ref.shape[2]
    for a in range(in_ref.shape[0]):
        for k in range(FIELDS):
            i, half = divmod(a * FIELDS + k, 2)
            half = pl.ds(half * EDGE, EDGE)
            one, two = one_ref[i, half, :], two_ref[i, half, :]
            state_ref[a, k, pl.ds(0, EDGE), :] = jnp.where(rotor, one, two)
            state_ref[a, k, pl.ds(EDGE, rows), :] = in_ref[a, k]
            state_ref[a, k, pl.ds(EDGE + rows, EDGE), :] = jnp.where(rotor, two, one)
    co = coefficients(segment, cycle_cells)
    write_sends(state_ref, co, *sends)


def local_kernel(cycle_cells, code_ref, old_ref, now_ref, base_ref, nxt_s, prv_s, up_s, dn_s):
    segments = now_ref.shape[0]
    step, segment, _ = decode(code_ref, segments)
    co = coefficients(segment, cycle_cells)
    lane, place = lanes_of()
    low = lane < HALF
    pairs = now_ref.shape[0]
    blocks = now_ref.shape[2] // SUB
    at_inner, at_outer = segment == 0, segment == segments - 1
    is_inner, is_outer = place == 0, place == HALF - 1
    low_half, low_weight = 0.5 * (co["r"] - 1.0), co["r"] - 0.5
    high_half, high_weight = 0.5 * (co["r"] + 1.0), co["r"] + 0.5
    zero = jnp.zeros((SUB, LANES), jnp.float32)
    low_half = jnp.where(at_inner, low_half, zero)
    low_weight = jnp.where(at_inner, low_weight, zero)
    high_half = jnp.where(at_outer, high_half, zero)
    high_weight = jnp.where(at_outer, high_weight, zero)
    rows_end = blocks * SUB
    for k in range(FIELDS):
        nxt_s[k, pl.ds(0, SUB), :] = zero
        prv_s[k, pl.ds(rows_end, SUB), :] = zero

    def pair(a, carry):
        for b in range(blocks):
            rows = pl.ds(b * SUB, SUB)
            c = cell([now_ref[a, k, rows, :] for k in range(FIELDS)])
            to_out, to_in = radial_terms(c, co)
            inner = wall_terms(c, low_half, low_weight, 1.0)
            outer = wall_terms(c, high_half, high_weight, -1.0)
            centre = centre_terms(c, co)
            nxt, prv = theta_terms(c, co)
            above, below = axial_terms(c)
            for k in range(FIELDS):
                inside = jnp.where(is_inner, inner[k], pltpu.roll(to_out[k], 1, 1))
                outside = jnp.where(is_outer, outer[k], pltpu.roll(to_in[k], LANES - 1, 1))
                total = co["inv_r"] * (inside + outside)
                if centre[k] is not None:
                    total = total + centre[k]
                nxt_s[k, pl.ds(b * SUB + SUB, SUB), :] = nxt[k]
                prv_s[k, rows, :] = prv[k]
                swapped_up = pltpu.roll(above[k], HALF, 1)
                swapped_dn = pltpu.roll(below[k], HALF, 1)
                total = total + jnp.where(low, swapped_dn, swapped_up)
                base_ref[a, k, rows, :] = total
                up_s[a, k, rows, :] = swapped_up
                dn_s[a, k, rows, :] = swapped_dn
        for b in range(blocks):
            rows = pl.ds(b * SUB, SUB)
            for k in range(FIELDS):
                base_ref[a, k, rows, :] = (
                    base_ref[a, k, rows, :]
                    + nxt_s[k, pl.ds(b * SUB + SUB - 1, SUB), :]
                    + prv_s[k, pl.ds(b * SUB + 1, SUB), :]
                )
        return carry

    lax.fori_loop(0, pairs, pair, 0)
    old_w, now_w, rate_w = weights_of(step)

    def finish(a, carry):
        lower = jnp.maximum(a - 1, 0)
        upper = jnp.minimum(a + 1, pairs - 1)
        has_upper = a < pairs - 1
        first = a == 0
        for b in range(blocks):
            rows = pl.ds(b * SUB, SUB)
            for k in range(FIELDS):
                from_below = up_s[lower, k, rows, :]
                from_below = jnp.where(first, pltpu.roll(from_below, HALF, 1), from_below)
                from_above = jnp.where(has_upper, dn_s[upper, k, rows, :], zero)
                rate = base_ref[a, k, rows, :] + jnp.where(low, from_below, from_above)
                base_ref[a, k, rows, :] = (
                    old_w * old_ref[a, k, rows, :] + now_w * now_ref[a, k, rows, :] + rate_w * rate
                )
        return carry

    lax.fori_loop(0, pairs, finish, 0)


def join_kernel(cycle_cells, code_ref, offsets_ref, base_ref, turn_ref, turn2_ref, inside_ref,
                outside_ref, state_ref, own_ref, *sends):
    step, segment, rotor = decode(code_ref, base_ref.shape[0])
    co = coefficients(segment, cycle_cells)
    _, _, rate_w = weights_of(step)
    lane, place = lanes_of()
    pairs = base_ref.shape[0]
    blocks = base_ref.shape[2] // SUB
    rows_all = blocks * SUB
    tile = own_ref.shape[2]
    rest = lax.rem(offsets_ref[0], tile)
    split = jnp.where(rotor, tile + EDGE - rest, EDGE + rest)
    shift = jnp.where(rotor, lax.rem(rows_all - rest, rows_all), rest)
    shift2 = jnp.where(rotor, tile - rest, rest + rows_all - tile)
    row_id = lax.broadcasted_iota(jnp.int32, (rows_all, LANES), 0)
    from_first = (row_id >= split) != rotor
    upper_half = lax.broadcasted_iota(jnp.int32, (rows_all, LANES), 1) >= HALF
    weight_r = rate_w * co["inv_r"]
    at_low = jnp.where(place == 0, weight_r, 0.0)
    at_high = jnp.where(place == HALF - 1, weight_r, 0.0)

    def opened(value):
        both = jnp.concatenate([pltpu.roll(value, HALF, 1), value], axis=0)
        return both[:rows_all]

    for b in range(blocks):
        rows = pl.ds(b * SUB, SUB)
        inside, outside = inside_ref[rows, :], outside_ref[rows, :]
        for a in range(pairs):
            for k in range(FIELDS):
                j = a * FIELDS + k
                moved = pltpu.roll(inside, LANES - j, 1) if j else inside
                value = base_ref[a, k, rows, :] + at_low * moved
                value = value + at_high * pltpu.roll(outside, HALF - 1 - j, 1)
                state_ref[a, k, rows, :] = value
    for k in range(FIELDS):
        mixed = jnp.where(
            from_first,
            pltpu.roll(opened(turn_ref[k]), shift, 0),
            pltpu.roll(opened(turn2_ref[k]), shift2, 0),
        )
        turned = jnp.where(upper_half, mixed, 0.0)
        signed = -rate_w if k == 3 else rate_w
        state_ref[pairs - 1, k] = state_ref[pairs - 1, k] + signed * turned

    @pl.when(step < 2)
    def _():
        write_sends(state_ref, co, *sends)

    @pl.when(step == 2)
    def _():
        for a in range(pairs):
            for k in range(FIELDS):
                own_ref[a, k] = state_ref[a, k, pl.ds(EDGE, tile), :]


def body(density, velocity, pressure, offsets):
    n_ax, n_az = lax.axis_size("ax"), lax.axis_size("az")
    planes, tile, cells = density.shape[1:]
    cycle_cells = tile * n_az

    vmem = pl.BlockSpec(memory_space=pltpu.VMEM)
    smem = pl.BlockSpec(memory_space=pltpu.SMEM)
    struct = lambda *shape: jax.ShapeDtypeStruct(shape, jnp.float32)
    tall = tile + 2 * EDGE
    block = struct(n_ax, FIELDS, tall, LANES)
    own = struct(n_ax, FIELDS, tile, LANES)
    outer_rows = struct(n_ax * FIELDS // 2, 2 * EDGE, LANES)
    half_rows = -(-(tall // SUB) // 2) * SUB
    sends = (struct(FIELDS, half_rows, LANES), struct(tall, LANES), struct(tall, LANES))

    def device(row, ax, az):
        return (row * n_ax + ax) * n_az + az

    every = [(row, ax, az) for row in range(2) for ax in range(n_ax) for az in range(n_az)]

    def along_ax(by):
        return [
            (device(r, x, z), device(r, x + by, z)) for r, x, z in every if 0 <= x + by < n_ax
        ]

    def turned(by):
        pairs = []
        for x in range(n_ax):
            for z in range(n_az):
                pairs.append((device(1, x, (z + by) % n_az), device(0, x, z)))
                pairs.append((device(0, x, z), device(1, x, (z + by) % n_az)))
        return pairs

    near = [(device(r, x, z), device(r, x, (z + (1 if r else -1)) % n_az)) for r, x, z in every]

    def call(kernel, outs, n_smem, n_vmem, scratch=()):
        return pl.pallas_call(
            kernel,
            out_shape=outs,
            in_specs=[smem] * n_smem + [vmem] * n_vmem,
            out_specs=jax.tree.map(lambda _: vmem, outs),
            scratch_shapes=list(scratch),
            cost_estimate=pl.CostEstimate(
                flops=8_000_000, bytes_accessed=3_000_000, transcendentals=0
            ),
        )

    kernel_of = lambda kernel: functools.partial(kernel, cycle_cells)
    taller = pltpu.VMEM((FIELDS, tall + SUB, LANES), jnp.float32)
    whole = pltpu.VMEM(block.shape, jnp.float32)

    chunks = call(pack_kernel, own, 0, 3)(density[0], velocity[0], pressure[0])
    whole_tile = lax.all_to_all(chunks, "ax", 0, 0, tiled=True)

    code = 4 * ((1 - lax.axis_index("row")) * n_ax + lax.axis_index("ax"))
    code_1 = jnp.reshape(code, (1,))
    packed = offsets[0] + cycle_cells * (offsets[1] + cycle_cells * offsets[2])
    up_rows, down_rows = call(edge_kernel, (outer_rows, outer_rows), 1, 1)(code_1, whole_tile)
    up_rows = lax.ppermute(up_rows, AXES, turned(1))
    down_rows = lax.ppermute(down_rows, AXES, near)
    up_rows = lax.ppermute(up_rows, AXES, turned(0))
    start, *first = call(kernel_of(first_kernel), (block, *sends), 1, 3)(
        code_1, whole_tile, up_rows, down_rows
    )
    carry = (start, whole_tile, *first)

    def branch(by):
        def run(up, out, inn):
            return (
                lax.ppermute(up, AXES, turned(by)),
                lax.ppermute(out, AXES, along_ax(1)),
                lax.ppermute(inn, AXES, along_ax(-1)),
            )
        return run

    def substep(_, carry):
        now, _, *edges, code, packed = carry
        index = lax.div(lax.rem(packed, cycle_cells), tile)
        code_1, left = jnp.reshape(code, (1,)), jnp.reshape(packed, (1,))
        turn1, inside, outside = lax.switch(
            index, [branch(by) for by in range(n_az)], *edges
        )
        turn2 = lax.ppermute(turn1, AXES, near)
        base = call(kernel_of(local_kernel), block, 1, 2, (taller, taller, whole, whole))(
            code_1, start, now
        )
        state = call(kernel_of(join_kernel), (block, own, *sends), 2, 5)(
            code_1, left, base, turn1, turn2, inside, outside
        )
        return (*state, code + 1, lax.div(packed, cycle_cells))

    carry = (*carry, code, packed)
    carry = lax.fori_loop(0, 3, substep, carry)
    chunks = lax.all_to_all(carry[1], "ax", 0, 0, tiled=True)
    return call(unpack_kernel, struct(FIELDS, planes, tile, cells), 0, 1)(chunks)[None]


def solution(mesh):
    placed = (
        P("row", "ax", "az", None),
        P("row", None, "ax", "az", None),
        P("row", "ax", "az", None),
        P(),
    )
    return jax.shard_map(
        body,
        mesh=mesh,
        in_specs=placed,
        out_specs=P("row", None, "ax", "az", None),
        check_vma=False,
    )
```

```python
import functools
import math

import jax
import jax.numpy as jnp
from jax import lax
from jax.experimental import pallas as pl
from jax.experimental.pallas import tpu as pltpu
from jax.sharding import PartitionSpec as P

HEAT_RATIO = 1.4
VISCOSITY = 0.8
CONDUCTION = 0.6
TIME_STEP = 0.1
AXIAL_CURVE = 4.0
AXES = ("row", "ax", "az")
FIELDS = 5
SUB = 8
LANES = 128
HALF = 64
EDGE = 4


def cell(state):
    rho, mt, mr, mz, energy = state
    inv = 1.0 / rho
    vt, vr, vz = mt * inv, mr * inv, mz * inv
    tt, rr, zz = mt * vt, mr * vr, mz * vz
    press = (HEAT_RATIO - 1.0) * (energy - 0.5 * (tt + rr + zz))
    visc = (
        None,
        VISCOSITY * vt,
        VISCOSITY * vr,
        VISCOSITY * vz,
        CONDUCTION * (press * inv),
    )
    return dict(
        mt=mt, mr=mr, mz=mz, vt=vt, vr=vr, vz=vz, tt=tt, rr=rr, zz=zz,
        tr=mt * vr, tz=mt * vz, rz=mr * vz, press=press, enth=energy + press, visc=visc,
    )


def flux_theta(c):
    return (c["mt"], c["tt"] + c["press"], c["tr"], c["tz"], c["enth"] * c["vt"])


def flux_radial(c):
    return (c["mr"], c["tr"], c["rr"] + c["press"], c["rz"], c["enth"] * c["vr"])


def flux_axial(c):
    return (c["mz"], c["tz"], c["rz"], c["zz"] + c["press"], c["enth"] * c["vz"])


def axial_terms(c):
    above, below = [], []
    for flux, visc in zip(flux_axial(c), c["visc"]):
        if visc is None:
            above.append(flux)
            below.append(-flux)
        else:
            side = AXIAL_CURVE * visc
            above.append(side + flux)
            below.append(side - flux)
    return above, below


def theta_terms(c, co):
    flux = [co["half_arc"] * f for f in flux_theta(c)]
    flux[1] = flux[1] - co["cross"] * c["visc"][2]
    flux[2] = flux[2] + co["cross"] * c["visc"][1]
    nxt, prv = [flux[0]], [-flux[0]]
    for k in range(1, FIELDS):
        side = co["arc2"] * c["visc"][k]
        nxt.append(side + flux[k])
        prv.append(side - flux[k])
    return nxt, prv


def radial_terms(c, co):
    out, inn = [], []
    for flux, visc in zip(flux_radial(c), c["visc"]):
        odd = co["half_r"] * flux
        if visc is None:
            out.append(odd)
            inn.append(-odd)
        else:
            odd = odd + 0.5 * visc
            even = co["r"] * visc
            out.append(even + odd)
            inn.append(even - odd)
    return out, inn


def wall_terms(c, half_rg, weight, sign):
    flux = flux_radial(c)
    signs = (-1.0, 1.0, 1.0, 1.0, -1.0)
    out = []
    for k in range(FIELDS):
        term = (sign * signs[k]) * (half_rg * flux[k])
        if k:
            term = term + (1.0 if k == 4 else -1.0) * (weight * c["visc"][k])
        out.append(term)
    return out


def centre_terms(c, co):
    centre = [None] + [-(co["centre"] * v) for v in c["visc"][1:]]
    centre[1] = centre[1] - co["inv_r"] * (c["tr"] + co["inv_r"] * c["visc"][1])
    centre[2] = centre[2] + co["inv_r"] * (c["tt"] + c["press"] - co["inv_r"] * c["visc"][2])
    return centre


def lanes_of():
    lane = lax.broadcasted_iota(jnp.int32, (SUB, LANES), 1)
    return lane, jnp.where(lane < HALF, lane, lane - HALF)


def coefficients(segment, cycle_cells):
    dtheta = 2.0 * math.pi / cycle_cells
    cells = (lanes_of()[1] + segment * HALF).astype(jnp.float32)
    r = cycle_cells / (2.0 * math.pi) + cells + 0.5
    inv_r = 1.0 / r
    arc2 = 1.0 / ((r * dtheta) * (r * dtheta))
    return dict(
        r=r, half_r=0.5 * r, inv_r=inv_r, half_arc=1.0 / (2.0 * r * dtheta), arc2=arc2,
        cross=1.0 / (r * r * dtheta), centre=2.0 * arc2 + 2.0 + 2.0 * AXIAL_CURVE,
    )


def weights_of(step):
    first, second = step == 0, step == 1
    old = jnp.where(first, 0.0, jnp.where(second, 0.75, 1.0 / 3.0))
    now = jnp.where(first, 1.0, jnp.where(second, 0.25, 2.0 / 3.0))
    return old, now, now * TIME_STEP


def decode(code_ref, segments):
    code = code_ref[0]
    place = lax.div(code, 4)
    return lax.rem(code, 4), lax.rem(place, segments), lax.div(place, segments) == 1


def pack_kernel(rho_ref, vel_ref, press_ref, out_ref):
    lane, _ = lanes_of()
    low = lane < HALF
    for b in range(rho_ref.shape[1] // SUB):
        rows = pl.ds(b * SUB, SUB)
        for w in range(rho_ref.shape[2] // LANES):
            cols = pl.ds(w * LANES, LANES)
            both = []
            for p in range(2):
                rho = rho_ref[p, rows, cols]
                vel = [vel_ref[d, p, rows, cols] for d in range(3)]
                square = vel[0] * vel[0] + vel[1] * vel[1] + vel[2] * vel[2]
                energy = press_ref[p, rows, cols] / (HEAT_RATIO - 1.0) + 0.5 * rho * square
                both.append([rho] + [rho * v for v in vel] + [energy])
            for k in range(FIELDS):
                first, second = both[0][k], both[1][k]
                out_ref[2 * w, k, rows, :] = jnp.where(low, first, pltpu.roll(second, HALF, 1))
                out_ref[2 * w + 1, k, rows, :] = jnp.where(low, pltpu.roll(first, HALF, 1), second)


def edge_kernel(code_ref, in_ref, up_ref, down_ref):
    front = lax.broadcasted_iota(jnp.int32, (SUB, LANES), 0) < EDGE
    _, _, rotor = decode(code_ref, in_ref.shape[0])
    end = pl.ds(in_ref.shape[2] - SUB, SUB)
    for i in range(up_ref.shape[0]):
        one, two = divmod(2 * i, FIELDS), divmod(2 * i + 1, FIELDS)
        head = jnp.where(
            front, in_ref[*one, pl.ds(0, SUB), :], pltpu.roll(in_ref[*two, pl.ds(0, SUB), :], EDGE, 0)
        )
        tail = jnp.where(front, pltpu.roll(in_ref[*one, end, :], EDGE, 0), in_ref[*two, end, :])
        up_ref[i] = jnp.where(rotor, tail, head)
        down_ref[i] = jnp.where(rotor, head, tail)


def unpack_kernel(in_ref, out_ref):
    lane, _ = lanes_of()
    low = lane < HALF
    for b in range(out_ref.shape[2] // SUB):
        rows = pl.ds(b * SUB, SUB)
        for w in range(in_ref.shape[0] // 2):
            cols = pl.ds(w * LANES, LANES)
            for k in range(FIELDS):
                inner, outer = in_ref[2 * w, k, rows, :], in_ref[2 * w + 1, k, rows, :]
                out_ref[k, 0, rows, cols] = jnp.where(low, inner, pltpu.roll(outer, HALF, 1))
                out_ref[k, 1, rows, cols] = jnp.where(low, pltpu.roll(inner, HALF, 1), outer)


def write_sends(state_ref, co, up_ref, out_ref, inn_ref):
    lane, place = lanes_of()
    pairs = state_ref.shape[0]
    blocks = state_ref.shape[2] // SUB
    top = []
    for b in range(blocks):
        rows = pl.ds(b * SUB, SUB)
        packed_out = jnp.zeros((SUB, LANES), jnp.float32)
        packed_in = jnp.zeros((SUB, LANES), jnp.float32)
        for a in range(pairs):
            c = cell([state_ref[a, k, rows, :] for k in range(FIELDS)])
            to_out, to_in = radial_terms(c, co)
            for k in range(FIELDS):
                j = a * FIELDS + k
                here = place == j
                moved = pltpu.roll(to_out[k], (j + 1 - HALF) % LANES, 1)
                packed_out = jnp.where(here, moved, packed_out)
                moved = pltpu.roll(to_in[k], j, 1) if j else to_in[k]
                packed_in = jnp.where(here, moved, packed_in)
            if a == pairs - 1:
                top.append(axial_terms(c)[0])
        out_ref[rows, :] = packed_out
        inn_ref[rows, :] = packed_in
    half = up_ref.shape[1] // SUB
    for b in range(half):
        for k in range(FIELDS):
            value = pltpu.roll(top[b][k], HALF, 1)
            if b + half < blocks:
                value = jnp.where(lane < HALF, value, top[b + half][k])
            up_ref[k, pl.ds(b * SUB, SUB), :] = value


def first_kernel(cycle_cells, code_ref, in_ref, one_ref, two_ref, state_ref, *sends):
    _, segment, rotor = decode(code_ref, in_ref.shape[0])
    rows = in_ref.shape[2]
    for a in range(in_ref.shape[0]):
        for k in range(FIELDS):
            i, half = divmod(a * FIELDS + k, 2)
            half = pl.ds(half * EDGE, EDGE)
            one, two = one_ref[i, half, :], two_ref[i, half, :]
            state_ref[a, k, pl.ds(0, EDGE), :] = jnp.where(rotor, one, two)
            state_ref[a, k, pl.ds(EDGE, rows), :] = in_ref[a, k]
            state_ref[a, k, pl.ds(EDGE + rows, EDGE), :] = jnp.where(rotor, two, one)
    co = coefficients(segment, cycle_cells)
    write_sends(state_ref, co, *sends)


def local_kernel(cycle_cells, code_ref, old_ref, now_ref, base_ref, nxt_s, prv_s, up_s, dn_s):
    segments = now_ref.shape[0]
    step, segment, _ = decode(code_ref, segments)
    co = coefficients(segment, cycle_cells)
    lane, place = lanes_of()
    low = lane < HALF
    pairs = now_ref.shape[0]
    blocks = now_ref.shape[2] // SUB
    at_inner, at_outer = segment == 0, segment == segments - 1
    is_inner, is_outer = place == 0, place == HALF - 1
    low_half, low_weight = 0.5 * (co["r"] - 1.0), co["r"] - 0.5
    high_half, high_weight = 0.5 * (co["r"] + 1.0), co["r"] + 0.5
    zero = jnp.zeros((SUB, LANES), jnp.float32)
    low_half = jnp.where(at_inner, low_half, zero)
    low_weight = jnp.where(at_inner, low_weight, zero)
    high_half = jnp.where(at_outer, high_half, zero)
    high_weight = jnp.where(at_outer, high_weight, zero)
    rows_end = blocks * SUB
    for k in range(FIELDS):
        nxt_s[k, pl.ds(0, SUB), :] = zero
        prv_s[k, pl.ds(rows_end, SUB), :] = zero

    def pair(a, carry):
        for b in range(blocks):
            rows = pl.ds(b * SUB, SUB)
            c = cell([now_ref[a, k, rows, :] for k in range(FIELDS)])
            to_out, to_in = radial_terms(c, co)
            inner = wall_terms(c, low_half, low_weight, 1.0)
            outer = wall_terms(c, high_half, high_weight, -1.0)
            centre = centre_terms(c, co)
            nxt, prv = theta_terms(c, co)
            above, below = axial_terms(c)
            for k in range(FIELDS):
                inside = jnp.where(is_inner, inner[k], pltpu.roll(to_out[k], 1, 1))
                outside = jnp.where(is_outer, outer[k], pltpu.roll(to_in[k], LANES - 1, 1))
                total = co["inv_r"] * (inside + outside)
                if centre[k] is not None:
                    total = total + centre[k]
                nxt_s[k, pl.ds(b * SUB + SUB, SUB), :] = nxt[k]
                prv_s[k, rows, :] = prv[k]
                swapped_up = pltpu.roll(above[k], HALF, 1)
                swapped_dn = pltpu.roll(below[k], HALF, 1)
                total = total + jnp.where(low, swapped_dn, swapped_up)
                base_ref[a, k, rows, :] = total
                up_s[a, k, rows, :] = swapped_up
                dn_s[a, k, rows, :] = swapped_dn
        for b in range(blocks):
            rows = pl.ds(b * SUB, SUB)
            for k in range(FIELDS):
                base_ref[a, k, rows, :] = (
                    base_ref[a, k, rows, :]
                    + nxt_s[k, pl.ds(b * SUB + SUB - 1, SUB), :]
                    + prv_s[k, pl.ds(b * SUB + 1, SUB), :]
                )
        return carry

    lax.fori_loop(0, pairs, pair, 0)
    old_w, now_w, rate_w = weights_of(step)

    def finish(a, carry):
        lower = jnp.maximum(a - 1, 0)
        upper = jnp.minimum(a + 1, pairs - 1)
        has_upper = a < pairs - 1
        first = a == 0
        for b in range(blocks):
            rows = pl.ds(b * SUB, SUB)
            for k in range(FIELDS):
                from_below = up_s[lower, k, rows, :]
                from_below = jnp.where(first, pltpu.roll(from_below, HALF, 1), from_below)
                from_above = jnp.where(has_upper, dn_s[upper, k, rows, :], zero)
                rate = base_ref[a, k, rows, :] + jnp.where(low, from_below, from_above)
                base_ref[a, k, rows, :] = (
                    old_w * old_ref[a, k, rows, :] + now_w * now_ref[a, k, rows, :] + rate_w * rate
                )
        return carry

    lax.fori_loop(0, pairs, finish, 0)


def join_kernel(cycle_cells, code_ref, offsets_ref, base_ref, turn_ref, turn2_ref, inside_ref,
                outside_ref, state_ref, *sends):
    step, segment, rotor = decode(code_ref, base_ref.shape[0])
    co = coefficients(segment, cycle_cells)
    _, _, rate_w = weights_of(step)
    lane, place = lanes_of()
    pairs = base_ref.shape[0]
    blocks = base_ref.shape[2] // SUB
    rows_all = blocks * SUB
    tile = rows_all - 2 * EDGE
    rest = lax.rem(offsets_ref[0], tile)
    split = jnp.where(rotor, tile + EDGE - rest, EDGE + rest)
    shift = jnp.where(rotor, lax.rem(rows_all - rest, rows_all), rest)
    shift2 = jnp.where(rotor, tile - rest, rest + rows_all - tile)
    row_id = lax.broadcasted_iota(jnp.int32, (rows_all, LANES), 0)
    from_first = (row_id >= split) != rotor
    upper_half = lax.broadcasted_iota(jnp.int32, (rows_all, LANES), 1) >= HALF
    weight_r = rate_w * co["inv_r"]
    at_low = jnp.where(place == 0, weight_r, 0.0)
    at_high = jnp.where(place == HALF - 1, weight_r, 0.0)

    def opened(value):
        both = jnp.concatenate([pltpu.roll(value, HALF, 1), value], axis=0)
        return both[:rows_all]

    for b in range(blocks):
        rows = pl.ds(b * SUB, SUB)
        inside, outside = inside_ref[rows, :], outside_ref[rows, :]
        for a in range(pairs):
            for k in range(FIELDS):
                j = a * FIELDS + k
                moved = pltpu.roll(inside, LANES - j, 1) if j else inside
                value = base_ref[a, k, rows, :] + at_low * moved
                value = value + at_high * pltpu.roll(outside, HALF - 1 - j, 1)
                state_ref[a, k, rows, :] = value
    for k in range(FIELDS):
        mixed = jnp.where(
            from_first,
            pltpu.roll(opened(turn_ref[k]), shift, 0),
            pltpu.roll(opened(turn2_ref[k]), shift2, 0),
        )
        turned = jnp.where(upper_half, mixed, 0.0)
        signed = -rate_w if k == 3 else rate_w
        state_ref[pairs - 1, k] = state_ref[pairs - 1, k] + signed * turned
    write_sends(state_ref, co, *sends)


def body(density, velocity, pressure, offsets):
    n_ax, n_az = lax.axis_size("ax"), lax.axis_size("az")
    planes, tile, cells = density.shape[1:]
    cycle_cells = tile * n_az

    vmem = pl.BlockSpec(memory_space=pltpu.VMEM)
    smem = pl.BlockSpec(memory_space=pltpu.SMEM)
    struct = lambda *shape: jax.ShapeDtypeStruct(shape, jnp.float32)
    tall = tile + 2 * EDGE
    block = struct(n_ax, FIELDS, tall, LANES)
    own = struct(n_ax, FIELDS, tile, LANES)
    outer_rows = struct(n_ax * FIELDS // 2, 2 * EDGE, LANES)
    half_rows = -(-(tall // SUB) // 2) * SUB
    sends = (struct(FIELDS, half_rows, LANES), struct(tall, LANES), struct(tall, LANES))

    def device(row, ax, az):
        return (row * n_ax + ax) * n_az + az

    every = [(row, ax, az) for row in range(2) for ax in range(n_ax) for az in range(n_az)]

    def along_ax(by):
        return [
            (device(r, x, z), device(r, x + by, z)) for r, x, z in every if 0 <= x + by < n_ax
        ]

    def turned(by):
        pairs = []
        for x in range(n_ax):
            for z in range(n_az):
                pairs.append((device(1, x, (z + by) % n_az), device(0, x, z)))
                pairs.append((device(0, x, z), device(1, x, (z + by) % n_az)))
        return pairs

    near = [(device(r, x, z), device(r, x, (z + (1 if r else -1)) % n_az)) for r, x, z in every]

    def call(kernel, outs, n_smem, n_vmem, scratch=()):
        return pl.pallas_call(
            kernel,
            out_shape=outs,
            in_specs=[smem] * n_smem + [vmem] * n_vmem,
            out_specs=jax.tree.map(lambda _: vmem, outs),
            scratch_shapes=list(scratch),
            cost_estimate=pl.CostEstimate(
                flops=8_000_000, bytes_accessed=3_000_000, transcendentals=0
            ),
        )

    kernel_of = lambda kernel: functools.partial(kernel, cycle_cells)
    taller = pltpu.VMEM((FIELDS, tall + SUB, LANES), jnp.float32)
    whole = pltpu.VMEM(block.shape, jnp.float32)

    chunks = call(pack_kernel, own, 0, 3)(density[0], velocity[0], pressure[0])
    whole_tile = lax.all_to_all(chunks, "ax", 0, 0, tiled=True)

    code = 4 * ((1 - lax.axis_index("row")) * n_ax + lax.axis_index("ax"))
    code_1 = jnp.reshape(code, (1,))
    packed = offsets[0] + cycle_cells * (offsets[1] + cycle_cells * offsets[2])
    up_rows, down_rows = call(edge_kernel, (outer_rows, outer_rows), 1, 1)(code_1, whole_tile)
    up_rows = lax.ppermute(up_rows, AXES, turned(1))
    down_rows = lax.ppermute(down_rows, AXES, near)
    up_rows = lax.ppermute(up_rows, AXES, turned(0))
    start, *first = call(kernel_of(first_kernel), (block, *sends), 1, 3)(
        code_1, whole_tile, up_rows, down_rows
    )
    carry = (start, *first)

    def branch(by):
        def run(code, now, up, out, inn):
            turn1 = lax.ppermute(up, AXES, turned(by))
            turn2 = lax.ppermute(up, AXES, turned((by + 1) % n_az))
            inside = lax.ppermute(out, AXES, along_ax(1))
            outside = lax.ppermute(inn, AXES, along_ax(-1))
            base = call(kernel_of(local_kernel), block, 1, 2, (taller, taller, whole, whole))(
                code, start, now
            )
            return base, turn1, turn2, inside, outside
        return run

    def substep(_, carry):
        *cells_and_edges, code, packed = carry
        index = lax.div(lax.rem(packed, cycle_cells), tile)
        code_1, left = jnp.reshape(code, (1,)), jnp.reshape(packed, (1,))
        terms = lax.switch(
            index, [branch(by) for by in range(n_az)], code_1, *cells_and_edges
        )
        state = call(kernel_of(join_kernel), (block, *sends), 2, 5)(code_1, left, *terms)
        return (*state, code + 1, lax.div(packed, cycle_cells))

    carry = (*carry, code, packed)
    carry = lax.fori_loop(0, 3, substep, carry)
    chunks = lax.all_to_all(carry[0][:, :, EDGE : EDGE + tile], "ax", 0, 0, tiled=True)
    return call(unpack_kernel, struct(FIELDS, planes, tile, cells), 0, 1)(chunks)[None]


def solution(mesh):
    placed = (
        P("row", "ax", "az", None),
        P("row", None, "ax", "az", None),
        P("row", "ax", "az", None),
        P(),
    )
    return jax.shard_map(
        body,
        mesh=mesh,
        in_specs=placed,
        out_specs=P("row", None, "ax", "az", None),
        check_vma=False,
    )
```

```python
import functools
import math

import jax
import jax.numpy as jnp
from jax import lax
from jax.experimental import pallas as pl
from jax.experimental.pallas import tpu as pltpu
from jax.sharding import PartitionSpec as P

HEAT_RATIO = 1.4
VISCOSITY = 0.8
CONDUCTION = 0.6
TIME_STEP = 0.1
AXIAL_CURVE = 4.0
AXES = ("row", "ax", "az")
FIELDS = 5
SUB = 8
LANES = 128
HALF = 64
KERNEL_VMEM = 12 * 2**20
EDGE = 4


def cell(state):
    rho, mt, mr, mz, energy = state
    inv = 1.0 / rho
    vt, vr, vz = mt * inv, mr * inv, mz * inv
    tt, rr, zz = mt * vt, mr * vr, mz * vz
    press = (HEAT_RATIO - 1.0) * (energy - 0.5 * (tt + rr + zz))
    visc = (
        None,
        VISCOSITY * vt,
        VISCOSITY * vr,
        VISCOSITY * vz,
        CONDUCTION * (press * inv),
    )
    return dict(
        mt=mt, mr=mr, mz=mz, vt=vt, vr=vr, vz=vz, tt=tt, rr=rr, zz=zz,
        tr=mt * vr, tz=mt * vz, rz=mr * vz, press=press, enth=energy + press, visc=visc,
    )


def flux_theta(c):
    return (c["mt"], c["tt"] + c["press"], c["tr"], c["tz"], c["enth"] * c["vt"])


def flux_radial(c):
    return (c["mr"], c["tr"], c["rr"] + c["press"], c["rz"], c["enth"] * c["vr"])


def flux_axial(c):
    return (c["mz"], c["tz"], c["rz"], c["zz"] + c["press"], c["enth"] * c["vz"])


def axial_terms(c):
    above, below = [], []
    for flux, visc in zip(flux_axial(c), c["visc"]):
        if visc is None:
            above.append(flux)
            below.append(-flux)
        else:
            side = AXIAL_CURVE * visc
            above.append(side + flux)
            below.append(side - flux)
    return above, below


def theta_terms(c, co):
    flux = [co["half_arc"] * f for f in flux_theta(c)]
    flux[1] = flux[1] - co["cross"] * c["visc"][2]
    flux[2] = flux[2] + co["cross"] * c["visc"][1]
    nxt, prv = [flux[0]], [-flux[0]]
    for k in range(1, FIELDS):
        side = co["arc2"] * c["visc"][k]
        nxt.append(side + flux[k])
        prv.append(side - flux[k])
    return nxt, prv


def radial_terms(c, co):
    out, inn = [], []
    for flux, visc in zip(flux_radial(c), c["visc"]):
        odd = co["half_r"] * flux
        if visc is None:
            out.append(odd)
            inn.append(-odd)
        else:
            odd = odd + 0.5 * visc
            even = co["r"] * visc
            out.append(even + odd)
            inn.append(even - odd)
    return out, inn


def wall_terms(c, half_rg, weight, sign):
    flux = flux_radial(c)
    signs = (-1.0, 1.0, 1.0, 1.0, -1.0)
    out = []
    for k in range(FIELDS):
        term = (sign * signs[k]) * (half_rg * flux[k])
        if k:
            term = term + (1.0 if k == 4 else -1.0) * (weight * c["visc"][k])
        out.append(term)
    return out


def centre_terms(c, co):
    centre = [None] + [-(co["centre"] * v) for v in c["visc"][1:]]
    centre[1] = centre[1] - co["inv_r"] * (c["tr"] + co["inv_r"] * c["visc"][1])
    centre[2] = centre[2] + co["inv_r"] * (c["tt"] + c["press"] - co["inv_r"] * c["visc"][2])
    return centre


def lanes_of():
    lane = lax.broadcasted_iota(jnp.int32, (SUB, LANES), 1)
    return lane, jnp.where(lane < HALF, lane, lane - HALF)


def coefficients(segment, cycle_cells):
    dtheta = 2.0 * math.pi / cycle_cells
    cells = (lanes_of()[1] + segment * HALF).astype(jnp.float32)
    r = cycle_cells / (2.0 * math.pi) + cells + 0.5
    inv_r = 1.0 / r
    arc2 = 1.0 / ((r * dtheta) * (r * dtheta))
    return dict(
        r=r, half_r=0.5 * r, inv_r=inv_r, half_arc=1.0 / (2.0 * r * dtheta), arc2=arc2,
        cross=1.0 / (r * r * dtheta), centre=2.0 * arc2 + 2.0 + 2.0 * AXIAL_CURVE,
    )


def weights_of(step):
    first, second = step == 0, step == 1
    old = jnp.where(first, 0.0, jnp.where(second, 0.75, 1.0 / 3.0))
    now = jnp.where(first, 1.0, jnp.where(second, 0.25, 2.0 / 3.0))
    return old, now, now * TIME_STEP


def decode(code_ref, segments):
    code = code_ref[0]
    place = lax.div(code, 4)
    return lax.rem(code, 4), lax.rem(place, segments), lax.div(place, segments) == 1


def pack_kernel(rho_ref, vel_ref, press_ref, out_ref):
    lane, _ = lanes_of()
    low = lane < HALF
    for b in range(rho_ref.shape[1] // SUB):
        rows = pl.ds(b * SUB, SUB)
        for w in range(rho_ref.shape[2] // LANES):
            cols = pl.ds(w * LANES, LANES)
            both = []
            for p in range(2):
                rho = rho_ref[p, rows, cols]
                vel = [vel_ref[d, p, rows, cols] for d in range(3)]
                square = vel[0] * vel[0] + vel[1] * vel[1] + vel[2] * vel[2]
                energy = press_ref[p, rows, cols] / (HEAT_RATIO - 1.0) + 0.5 * rho * square
                both.append([rho] + [rho * v for v in vel] + [energy])
            for k in range(FIELDS):
                first, second = both[0][k], both[1][k]
                out_ref[2 * w, k, rows, :] = jnp.where(low, first, pltpu.roll(second, HALF, 1))
                out_ref[2 * w + 1, k, rows, :] = jnp.where(low, pltpu.roll(first, HALF, 1), second)


def edge_kernel(code_ref, in_ref, up_ref, down_ref):
    front = lax.broadcasted_iota(jnp.int32, (SUB, LANES), 0) < EDGE
    _, _, rotor = decode(code_ref, in_ref.shape[0])
    end = pl.ds(in_ref.shape[2] - SUB, SUB)
    for i in range(up_ref.shape[0]):
        one, two = divmod(2 * i, FIELDS), divmod(2 * i + 1, FIELDS)
        head = jnp.where(
            front, in_ref[*one, pl.ds(0, SUB), :], pltpu.roll(in_ref[*two, pl.ds(0, SUB), :], EDGE, 0)
        )
        tail = jnp.where(front, pltpu.roll(in_ref[*one, end, :], EDGE, 0), in_ref[*two, end, :])
        up_ref[i] = jnp.where(rotor, tail, head)
        down_ref[i] = jnp.where(rotor, head, tail)


def unpack_kernel(in_ref, out_ref):
    lane, _ = lanes_of()
    low = lane < HALF
    for b in range(out_ref.shape[2] // SUB):
        rows = pl.ds(b * SUB, SUB)
        for w in range(in_ref.shape[0] // 2):
            cols = pl.ds(w * LANES, LANES)
            for k in range(FIELDS):
                inner, outer = in_ref[2 * w, k, rows, :], in_ref[2 * w + 1, k, rows, :]
                out_ref[k, 0, rows, cols] = jnp.where(low, inner, pltpu.roll(outer, HALF, 1))
                out_ref[k, 1, rows, cols] = jnp.where(low, pltpu.roll(inner, HALF, 1), outer)


def write_sends(state_ref, co, segment, up_ref, one_ref, two_ref):
    odd = lax.rem(segment, 2) == 1
    lane, place = lanes_of()
    pairs = state_ref.shape[0]
    blocks = state_ref.shape[2] // SUB
    top = []
    for b in range(blocks):
        rows = pl.ds(b * SUB, SUB)
        packed_out = jnp.zeros((SUB, LANES), jnp.float32)
        packed_in = jnp.zeros((SUB, LANES), jnp.float32)
        for a in range(pairs):
            c = cell([state_ref[a, k, rows, :] for k in range(FIELDS)])
            to_out, to_in = radial_terms(c, co)
            for k in range(FIELDS):
                j = a * FIELDS + k
                here = place == j
                moved = pltpu.roll(to_out[k], (j + 1 - HALF) % LANES, 1)
                packed_out = jnp.where(here, moved, packed_out)
                moved = pltpu.roll(to_in[k], j, 1) if j else to_in[k]
                packed_in = jnp.where(here, moved, packed_in)
            if a == pairs - 1:
                top.append(axial_terms(c)[0])
        one_ref[rows, :] = jnp.where(odd, packed_in, packed_out)
        two_ref[rows, :] = jnp.where(odd, packed_out, packed_in)
    half = up_ref.shape[1] // SUB
    for b in range(half):
        for k in range(FIELDS):
            value = pltpu.roll(top[b][k], HALF, 1)
            if b + half < blocks:
                value = jnp.where(lane < HALF, value, top[b + half][k])
            up_ref[k, pl.ds(b * SUB, SUB), :] = value


def first_kernel(cycle_cells, code_ref, in_ref, one_ref, two_ref, state_ref, *sends):
    _, segment, rotor = decode(code_ref, in_ref.shape[0])
    rows = in_ref.shape[2]
    for a in range(in_ref.shape[0]):
        for k in range(FIELDS):
            i, half = divmod(a * FIELDS + k, 2)
            half = pl.ds(half * EDGE, EDGE)
            one, two = one_ref[i, half, :], two_ref[i, half, :]
            state_ref[a, k, pl.ds(0, EDGE), :] = jnp.where(rotor, one, two)
            state_ref[a, k, pl.ds(EDGE, rows), :] = in_ref[a, k]
            state_ref[a, k, pl.ds(EDGE + rows, EDGE), :] = jnp.where(rotor, two, one)
    co = coefficients(segment, cycle_cells)
    write_sends(state_ref, co, segment, *sends)


def local_kernel(cycle_cells, code_ref, old_ref, now_ref, base_ref, nxt_s, prv_s, up_s, dn_s):
    segments = now_ref.shape[0]
    step, segment, _ = decode(code_ref, segments)
    co = coefficients(segment, cycle_cells)
    lane, place = lanes_of()
    low = lane < HALF
    pairs = now_ref.shape[0]
    blocks = now_ref.shape[2] // SUB
    at_inner, at_outer = segment == 0, segment == segments - 1
    is_inner, is_outer = place == 0, place == HALF - 1
    low_half, low_weight = 0.5 * (co["r"] - 1.0), co["r"] - 0.5
    high_half, high_weight = 0.5 * (co["r"] + 1.0), co["r"] + 0.5
    zero = jnp.zeros((SUB, LANES), jnp.float32)
    low_half = jnp.where(at_inner, low_half, zero)
    low_weight = jnp.where(at_inner, low_weight, zero)
    high_half = jnp.where(at_outer, high_half, zero)
    high_weight = jnp.where(at_outer, high_weight, zero)
    rows_end = blocks * SUB
    for k in range(FIELDS):
        nxt_s[k, pl.ds(0, SUB), :] = zero
        prv_s[k, pl.ds(rows_end, SUB), :] = zero

    def pair(a, carry):
        for b in range(blocks):
            rows = pl.ds(b * SUB, SUB)
            c = cell([now_ref[a, k, rows, :] for k in range(FIELDS)])
            to_out, to_in = radial_terms(c, co)
            inner = wall_terms(c, low_half, low_weight, 1.0)
            outer = wall_terms(c, high_half, high_weight, -1.0)
            centre = centre_terms(c, co)
            nxt, prv = theta_terms(c, co)
            above, below = axial_terms(c)
            for k in range(FIELDS):
                inside = jnp.where(is_inner, inner[k], pltpu.roll(to_out[k], 1, 1))
                outside = jnp.where(is_outer, outer[k], pltpu.roll(to_in[k], LANES - 1, 1))
                total = co["inv_r"] * (inside + outside)
                if centre[k] is not None:
                    total = total + centre[k]
                nxt_s[k, pl.ds(b * SUB + SUB, SUB), :] = nxt[k]
                prv_s[k, rows, :] = prv[k]
                swapped_up = pltpu.roll(above[k], HALF, 1)
                swapped_dn = pltpu.roll(below[k], HALF, 1)
                total = total + jnp.where(low, swapped_dn, swapped_up)
                base_ref[a, k, rows, :] = total
                up_s[a, k, rows, :] = swapped_up
                dn_s[a, k, rows, :] = swapped_dn
        for b in range(blocks):
            rows = pl.ds(b * SUB, SUB)
            for k in range(FIELDS):
                base_ref[a, k, rows, :] = (
                    base_ref[a, k, rows, :]
                    + nxt_s[k, pl.ds(b * SUB + SUB - 1, SUB), :]
                    + prv_s[k, pl.ds(b * SUB + 1, SUB), :]
                )
        return carry

    lax.fori_loop(0, pairs, pair, 0)
    old_w, now_w, rate_w = weights_of(step)

    def finish(a, carry):
        lower = jnp.maximum(a - 1, 0)
        upper = jnp.minimum(a + 1, pairs - 1)
        has_upper = a < pairs - 1
        first = a == 0
        for b in range(blocks):
            rows = pl.ds(b * SUB, SUB)
            for k in range(FIELDS):
                from_below = up_s[lower, k, rows, :]
                from_below = jnp.where(first, pltpu.roll(from_below, HALF, 1), from_below)
                from_above = jnp.where(has_upper, dn_s[upper, k, rows, :], zero)
                rate = base_ref[a, k, rows, :] + jnp.where(low, from_below, from_above)
                base_ref[a, k, rows, :] = (
                    old_w * old_ref[a, k, rows, :] + now_w * now_ref[a, k, rows, :] + rate_w * rate
                )
        return carry

    lax.fori_loop(0, pairs, finish, 0)


def join_kernel(cycle_cells, code_ref, offsets_ref, base_ref, turn_ref, turn2_ref, one_ref,
                two_ref, state_ref, *sends):
    step, segment, rotor = decode(code_ref, base_ref.shape[0])
    co = coefficients(segment, cycle_cells)
    _, _, rate_w = weights_of(step)
    odd = lax.rem(segment, 2) == 1
    lane, place = lanes_of()
    pairs = base_ref.shape[0]
    blocks = base_ref.shape[2] // SUB
    rows_all = blocks * SUB
    tile = rows_all - 2 * EDGE
    rest = lax.rem(offsets_ref[0], tile)
    split = jnp.where(rotor, tile + EDGE - rest, EDGE + rest)
    shift = jnp.where(rotor, lax.rem(rows_all - rest, rows_all), rest)
    shift2 = jnp.where(rotor, tile - rest, rest + rows_all - tile)
    row_id = lax.broadcasted_iota(jnp.int32, (rows_all, LANES), 0)
    from_first = (row_id >= split) != rotor
    upper_half = lax.broadcasted_iota(jnp.int32, (rows_all, LANES), 1) >= HALF
    weight_r = rate_w * co["inv_r"]
    at_low = jnp.where(place == 0, weight_r, 0.0)
    at_high = jnp.where(place == HALF - 1, weight_r, 0.0)

    def opened(value):
        both = jnp.concatenate([pltpu.roll(value, HALF, 1), value], axis=0)
        return both[:rows_all]

    for b in range(blocks):
        rows = pl.ds(b * SUB, SUB)
        inside = jnp.where(odd, one_ref[rows, :], two_ref[rows, :])
        outside = jnp.where(odd, two_ref[rows, :], one_ref[rows, :])
        for a in range(pairs):
            for k in range(FIELDS):
                j = a * FIELDS + k
                moved = pltpu.roll(inside, LANES - j, 1) if j else inside
                value = base_ref[a, k, rows, :] + at_low * moved
                value = value + at_high * pltpu.roll(outside, HALF - 1 - j, 1)
                state_ref[a, k, rows, :] = value
    for k in range(FIELDS):
        mixed = jnp.where(
            from_first,
            pltpu.roll(opened(turn_ref[k]), shift, 0),
            pltpu.roll(opened(turn2_ref[k]), shift2, 0),
        )
        turned = jnp.where(upper_half, mixed, 0.0)
        signed = -rate_w if k == 3 else rate_w
        state_ref[pairs - 1, k] = state_ref[pairs - 1, k] + signed * turned
    write_sends(state_ref, co, segment, *sends)


def body(density, velocity, pressure, offsets):
    n_ax, n_az = lax.axis_size("ax"), lax.axis_size("az")
    planes, tile, cells = density.shape[1:]
    cycle_cells = tile * n_az

    vmem = pl.BlockSpec(memory_space=pltpu.VMEM)
    smem = pl.BlockSpec(memory_space=pltpu.SMEM)
    struct = lambda *shape: jax.ShapeDtypeStruct(shape, jnp.float32)
    tall = tile + 2 * EDGE
    block = struct(n_ax, FIELDS, tall, LANES)
    own = struct(n_ax, FIELDS, tile, LANES)
    outer_rows = struct(n_ax * FIELDS // 2, 2 * EDGE, LANES)
    half_rows = -(-(tall // SUB) // 2) * SUB
    sends = (struct(FIELDS, half_rows, LANES), struct(tall, LANES), struct(tall, LANES))

    def device(row, ax, az):
        return (row * n_ax + ax) * n_az + az

    every = [(row, ax, az) for row in range(2) for ax in range(n_ax) for az in range(n_az)]

    def swapped(first):
        partner = lambda x: x + 1 if (x - first) % 2 == 0 else x - 1
        return [
            (device(r, x, z), device(r, partner(x), z)) for r, x, z in every
            if 0 <= partner(x) < n_ax
        ]

    def turned(by):
        pairs = []
        for x in range(n_ax):
            for z in range(n_az):
                pairs.append((device(1, x, (z + by) % n_az), device(0, x, z)))
                pairs.append((device(0, x, z), device(1, x, (z + by) % n_az)))
        return pairs

    near = [(device(r, x, z), device(r, x, (z + (1 if r else -1)) % n_az)) for r, x, z in every]

    def call(kernel, outs, n_smem, n_vmem, scratch=()):
        return pl.pallas_call(
            kernel,
            out_shape=outs,
            in_specs=[smem] * n_smem + [vmem] * n_vmem,
            out_specs=jax.tree.map(lambda _: vmem, outs),
            scratch_shapes=list(scratch),
            compiler_params=pltpu.CompilerParams(vmem_limit_bytes=KERNEL_VMEM),
            cost_estimate=pl.CostEstimate(
                flops=8_000_000, bytes_accessed=3_000_000, transcendentals=0
            ),
        )

    kernel_of = lambda kernel: functools.partial(kernel, cycle_cells)
    taller = pltpu.VMEM((FIELDS, tall + SUB, LANES), jnp.float32)
    whole = pltpu.VMEM(block.shape, jnp.float32)

    chunks = call(pack_kernel, own, 0, 3)(density[0], velocity[0], pressure[0])
    whole_tile = lax.all_to_all(chunks, "ax", 0, 0, tiled=True)

    code = 4 * ((1 - lax.axis_index("row")) * n_ax + lax.axis_index("ax"))
    code_1 = jnp.reshape(code, (1,))
    packed = offsets[0] + cycle_cells * (offsets[1] + cycle_cells * offsets[2])
    up_rows, down_rows = call(edge_kernel, (outer_rows, outer_rows), 1, 1)(code_1, whole_tile)
    up_rows = lax.ppermute(up_rows, AXES, turned(1))
    down_rows = lax.ppermute(down_rows, AXES, near)
    up_rows = lax.ppermute(up_rows, AXES, turned(0))
    start, *first = call(kernel_of(first_kernel), (block, *sends), 1, 3)(
        code_1, whole_tile, up_rows, down_rows
    )
    carry = (start, *first)

    def branch(by):
        def run(code, now, up, one, two):
            turn1 = lax.ppermute(up, AXES, turned(by))
            turn2 = lax.ppermute(up, AXES, turned((by + 1) % n_az))
            one = lax.ppermute(one, AXES, swapped(0))
            two = lax.ppermute(two, AXES, swapped(1))
            base = call(kernel_of(local_kernel), block, 1, 2, (taller, taller, whole, whole))(
                code, start, now
            )
            return base, turn1, turn2, one, two
        return run

    def substep(_, carry):
        *cells_and_edges, code, packed = carry
        index = lax.div(lax.rem(packed, cycle_cells), tile)
        code_1, left = jnp.reshape(code, (1,)), jnp.reshape(packed, (1,))
        terms = lax.switch(
            index, [branch(by) for by in range(n_az)], code_1, *cells_and_edges
        )
        state = call(kernel_of(join_kernel), (block, *sends), 2, 5)(code_1, left, *terms)
        return (*state, code + 1, lax.div(packed, cycle_cells))

    carry = (*carry, code, packed)
    carry = lax.fori_loop(0, 3, substep, carry)
    chunks = lax.all_to_all(carry[0][:, :, EDGE : EDGE + tile], "ax", 0, 0, tiled=True)
    return call(unpack_kernel, struct(FIELDS, planes, tile, cells), 0, 1)(chunks)[None]


def solution(mesh):
    placed = (
        P("row", "ax", "az", None),
        P("row", None, "ax", "az", None),
        P("row", "ax", "az", None),
        P(),
    )
    return jax.shard_map(
        body,
        mesh=mesh,
        in_specs=placed,
        out_specs=P("row", None, "ax", "az", None),
        check_vma=False,
    )
```

```python
import functools
import math

import jax
import jax.numpy as jnp
from jax import lax
from jax.experimental import pallas as pl
from jax.experimental.pallas import tpu as pltpu
from jax.sharding import PartitionSpec as P

HEAT_RATIO = 1.4
VISCOSITY = 0.8
CONDUCTION = 0.6
TIME_STEP = 0.1
AXIAL_CURVE = 4.0
AXES = ("row", "ax", "az")
FIELDS = 5
SUB = 8
LANES = 128
HALF = 64
KERNEL_VMEM = 12 * 2**20
EDGE = 4


def cell(state):
    rho, mt, mr, mz, energy = state
    inv = 1.0 / rho
    vt, vr, vz = mt * inv, mr * inv, mz * inv
    tt, rr, zz = mt * vt, mr * vr, mz * vz
    press = (HEAT_RATIO - 1.0) * (energy - 0.5 * (tt + rr + zz))
    visc = (
        None,
        VISCOSITY * vt,
        VISCOSITY * vr,
        VISCOSITY * vz,
        CONDUCTION * (press * inv),
    )
    return dict(
        mt=mt, mr=mr, mz=mz, vt=vt, vr=vr, vz=vz, tt=tt, rr=rr, zz=zz,
        tr=mt * vr, tz=mt * vz, rz=mr * vz, press=press, enth=energy + press, visc=visc,
    )


def flux_theta(c):
    return (c["mt"], c["tt"] + c["press"], c["tr"], c["tz"], c["enth"] * c["vt"])


def flux_radial(c):
    return (c["mr"], c["tr"], c["rr"] + c["press"], c["rz"], c["enth"] * c["vr"])


def flux_axial(c):
    return (c["mz"], c["tz"], c["rz"], c["zz"] + c["press"], c["enth"] * c["vz"])


def axial_terms(c):
    above, below = [], []
    for flux, visc in zip(flux_axial(c), c["visc"]):
        if visc is None:
            above.append(flux)
            below.append(-flux)
        else:
            side = AXIAL_CURVE * visc
            above.append(side + flux)
            below.append(side - flux)
    return above, below


def theta_terms(c, co):
    flux = [co["half_arc"] * f for f in flux_theta(c)]
    flux[1] = flux[1] - co["cross"] * c["visc"][2]
    flux[2] = flux[2] + co["cross"] * c["visc"][1]
    nxt, prv = [flux[0]], [-flux[0]]
    for k in range(1, FIELDS):
        side = co["arc2"] * c["visc"][k]
        nxt.append(side + flux[k])
        prv.append(side - flux[k])
    return nxt, prv


def radial_terms(c, co):
    out, inn = [], []
    for flux, visc in zip(flux_radial(c), c["visc"]):
        odd = co["half_r"] * flux
        if visc is None:
            out.append(odd)
            inn.append(-odd)
        else:
            odd = odd + 0.5 * visc
            even = co["r"] * visc
            out.append(even + odd)
            inn.append(even - odd)
    return out, inn


def wall_terms(c, half_rg, weight, sign):
    flux = flux_radial(c)
    signs = (-1.0, 1.0, 1.0, 1.0, -1.0)
    out = []
    for k in range(FIELDS):
        term = (sign * signs[k]) * (half_rg * flux[k])
        if k:
            term = term + (1.0 if k == 4 else -1.0) * (weight * c["visc"][k])
        out.append(term)
    return out


def centre_terms(c, co):
    centre = [None] + [-(co["centre"] * v) for v in c["visc"][1:]]
    centre[1] = centre[1] - co["inv_r"] * (c["tr"] + co["inv_r"] * c["visc"][1])
    centre[2] = centre[2] + co["inv_r"] * (c["tt"] + c["press"] - co["inv_r"] * c["visc"][2])
    return centre


def lanes_of():
    lane = lax.broadcasted_iota(jnp.int32, (SUB, LANES), 1)
    return lane, jnp.where(lane < HALF, lane, lane - HALF)


def coefficients(segment, cycle_cells):
    dtheta = 2.0 * math.pi / cycle_cells
    cells = (lanes_of()[1] + segment * HALF).astype(jnp.float32)
    r = cycle_cells / (2.0 * math.pi) + cells + 0.5
    inv_r = 1.0 / r
    arc2 = 1.0 / ((r * dtheta) * (r * dtheta))
    return dict(
        r=r, half_r=0.5 * r, inv_r=inv_r, half_arc=1.0 / (2.0 * r * dtheta), arc2=arc2,
        cross=1.0 / (r * r * dtheta), centre=2.0 * arc2 + 2.0 + 2.0 * AXIAL_CURVE,
    )


def weights_of(step):
    first, second = step == 0, step == 1
    old = jnp.where(first, 0.0, jnp.where(second, 0.75, 1.0 / 3.0))
    now = jnp.where(first, 1.0, jnp.where(second, 0.25, 2.0 / 3.0))
    return old, now, now * TIME_STEP


def decode(code_ref, segments):
    code = code_ref[0]
    place = lax.div(code, 4)
    return lax.rem(code, 4), lax.rem(place, segments), lax.div(place, segments) == 1


def pack_kernel(rho_ref, vel_ref, press_ref, out_ref):
    lane, _ = lanes_of()
    low = lane < HALF
    for b in range(rho_ref.shape[1] // SUB):
        rows = pl.ds(b * SUB, SUB)
        for w in range(rho_ref.shape[2] // LANES):
            cols = pl.ds(w * LANES, LANES)
            both = []
            for p in range(2):
                rho = rho_ref[p, rows, cols]
                vel = [vel_ref[d, p, rows, cols] for d in range(3)]
                square = vel[0] * vel[0] + vel[1] * vel[1] + vel[2] * vel[2]
                energy = press_ref[p, rows, cols] / (HEAT_RATIO - 1.0) + 0.5 * rho * square
                both.append([rho] + [rho * v for v in vel] + [energy])
            for k in range(FIELDS):
                first, second = both[0][k], both[1][k]
                out_ref[2 * w, k, rows, :] = jnp.where(low, first, pltpu.roll(second, HALF, 1))
                out_ref[2 * w + 1, k, rows, :] = jnp.where(low, pltpu.roll(first, HALF, 1), second)


def edge_kernel(code_ref, in_ref, up_ref, down_ref):
    front = lax.broadcasted_iota(jnp.int32, (SUB, LANES), 0) < EDGE
    _, _, rotor = decode(code_ref, in_ref.shape[0])
    end = pl.ds(in_ref.shape[2] - SUB, SUB)
    for i in range(up_ref.shape[0]):
        one, two = divmod(2 * i, FIELDS), divmod(2 * i + 1, FIELDS)
        head = jnp.where(
            front, in_ref[*one, pl.ds(0, SUB), :], pltpu.roll(in_ref[*two, pl.ds(0, SUB), :], EDGE, 0)
        )
        tail = jnp.where(front, pltpu.roll(in_ref[*one, end, :], EDGE, 0), in_ref[*two, end, :])
        up_ref[i] = jnp.where(rotor, tail, head)
        down_ref[i] = jnp.where(rotor, head, tail)


def unpack_kernel(in_ref, out_ref):
    lane, _ = lanes_of()
    low = lane < HALF
    for b in range(out_ref.shape[2] // SUB):
        rows = pl.ds(b * SUB, SUB)
        for w in range(in_ref.shape[0] // 2):
            cols = pl.ds(w * LANES, LANES)
            for k in range(FIELDS):
                inner, outer = in_ref[2 * w, k, rows, :], in_ref[2 * w + 1, k, rows, :]
                out_ref[k, 0, rows, cols] = jnp.where(low, inner, pltpu.roll(outer, HALF, 1))
                out_ref[k, 1, rows, cols] = jnp.where(low, pltpu.roll(inner, HALF, 1), outer)


def write_sends(state_ref, co, segment, up_ref, one_ref, two_ref):
    odd = lax.rem(segment, 2) == 1
    lane, place = lanes_of()
    pairs = state_ref.shape[0]
    blocks = state_ref.shape[2] // SUB
    top = []
    for b in range(blocks):
        rows = pl.ds(b * SUB, SUB)
        packed_out = jnp.zeros((SUB, LANES), jnp.float32)
        packed_in = jnp.zeros((SUB, LANES), jnp.float32)
        for a in range(pairs):
            c = cell([state_ref[a, k, rows, :] for k in range(FIELDS)])
            to_out, to_in = radial_terms(c, co)
            for k in range(FIELDS):
                j = a * FIELDS + k
                here = place == j
                moved = pltpu.roll(to_out[k], (j + 1 - HALF) % LANES, 1)
                packed_out = jnp.where(here, moved, packed_out)
                moved = pltpu.roll(to_in[k], j, 1) if j else to_in[k]
                packed_in = jnp.where(here, moved, packed_in)
            if a == pairs - 1:
                top.append(axial_terms(c)[0])
        one_ref[rows, :] = jnp.where(odd, packed_in, packed_out)
        two_ref[rows, :] = jnp.where(odd, packed_out, packed_in)
    halves = [top[b][k] for k in range(FIELDS) for b in range(blocks)]
    for h in range(up_ref.shape[0]):
        value = pltpu.roll(halves[2 * h], HALF, 1)
        if 2 * h + 1 < len(halves):
            value = jnp.where(lane < HALF, value, halves[2 * h + 1])
        up_ref[h] = value


def first_kernel(cycle_cells, code_ref, in_ref, one_ref, two_ref, state_ref, *sends):
    _, segment, rotor = decode(code_ref, in_ref.shape[0])
    rows = in_ref.shape[2]
    for a in range(in_ref.shape[0]):
        for k in range(FIELDS):
            i, half = divmod(a * FIELDS + k, 2)
            half = pl.ds(half * EDGE, EDGE)
            one, two = one_ref[i, half, :], two_ref[i, half, :]
            state_ref[a, k, pl.ds(0, EDGE), :] = jnp.where(rotor, one, two)
            state_ref[a, k, pl.ds(EDGE, rows), :] = in_ref[a, k]
            state_ref[a, k, pl.ds(EDGE + rows, EDGE), :] = jnp.where(rotor, two, one)
    co = coefficients(segment, cycle_cells)
    write_sends(state_ref, co, segment, *sends)


def local_kernel(cycle_cells, code_ref, old_ref, now_ref, base_ref, nxt_s, prv_s, up_s, dn_s):
    segments = now_ref.shape[0]
    step, segment, _ = decode(code_ref, segments)
    co = coefficients(segment, cycle_cells)
    lane, place = lanes_of()
    low = lane < HALF
    pairs = now_ref.shape[0]
    blocks = now_ref.shape[2] // SUB
    at_inner, at_outer = segment == 0, segment == segments - 1
    is_inner, is_outer = place == 0, place == HALF - 1
    low_half, low_weight = 0.5 * (co["r"] - 1.0), co["r"] - 0.5
    high_half, high_weight = 0.5 * (co["r"] + 1.0), co["r"] + 0.5
    zero = jnp.zeros((SUB, LANES), jnp.float32)
    low_half = jnp.where(at_inner, low_half, zero)
    low_weight = jnp.where(at_inner, low_weight, zero)
    high_half = jnp.where(at_outer, high_half, zero)
    high_weight = jnp.where(at_outer, high_weight, zero)
    rows_end = blocks * SUB
    for k in range(FIELDS):
        nxt_s[k, pl.ds(0, SUB), :] = zero
        prv_s[k, pl.ds(rows_end, SUB), :] = zero

    def pair(a, carry):
        for b in range(blocks):
            rows = pl.ds(b * SUB, SUB)
            c = cell([now_ref[a, k, rows, :] for k in range(FIELDS)])
            to_out, to_in = radial_terms(c, co)
            inner = wall_terms(c, low_half, low_weight, 1.0)
            outer = wall_terms(c, high_half, high_weight, -1.0)
            centre = centre_terms(c, co)
            nxt, prv = theta_terms(c, co)
            above, below = axial_terms(c)
            for k in range(FIELDS):
                inside = jnp.where(is_inner, inner[k], pltpu.roll(to_out[k], 1, 1))
                outside = jnp.where(is_outer, outer[k], pltpu.roll(to_in[k], LANES - 1, 1))
                total = co["inv_r"] * (inside + outside)
                if centre[k] is not None:
                    total = total + centre[k]
                nxt_s[k, pl.ds(b * SUB + SUB, SUB), :] = nxt[k]
                prv_s[k, rows, :] = prv[k]
                swapped_up = pltpu.roll(above[k], HALF, 1)
                swapped_dn = pltpu.roll(below[k], HALF, 1)
                total = total + jnp.where(low, swapped_dn, swapped_up)
                base_ref[a, k, rows, :] = total
                up_s[a, k, rows, :] = swapped_up
                dn_s[a, k, rows, :] = swapped_dn
        for b in range(blocks):
            rows = pl.ds(b * SUB, SUB)
            for k in range(FIELDS):
                base_ref[a, k, rows, :] = (
                    base_ref[a, k, rows, :]
                    + nxt_s[k, pl.ds(b * SUB + SUB - 1, SUB), :]
                    + prv_s[k, pl.ds(b * SUB + 1, SUB), :]
                )
        return carry

    lax.fori_loop(0, pairs, pair, 0)
    old_w, now_w, rate_w = weights_of(step)

    def finish(a, carry):
        lower = jnp.maximum(a - 1, 0)
        upper = jnp.minimum(a + 1, pairs - 1)
        has_upper = a < pairs - 1
        first = a == 0
        for b in range(blocks):
            rows = pl.ds(b * SUB, SUB)
            for k in range(FIELDS):
                from_below = up_s[lower, k, rows, :]
                from_below = jnp.where(first, pltpu.roll(from_below, HALF, 1), from_below)
                from_above = jnp.where(has_upper, dn_s[upper, k, rows, :], zero)
                rate = base_ref[a, k, rows, :] + jnp.where(low, from_below, from_above)
                base_ref[a, k, rows, :] = (
                    old_w * old_ref[a, k, rows, :] + now_w * now_ref[a, k, rows, :] + rate_w * rate
                )
        return carry

    lax.fori_loop(0, pairs, finish, 0)


def join_kernel(cycle_cells, code_ref, offsets_ref, base_ref, turn_ref, turn2_ref, one_ref,
                two_ref, state_ref, *sends):
    step, segment, rotor = decode(code_ref, base_ref.shape[0])
    co = coefficients(segment, cycle_cells)
    _, _, rate_w = weights_of(step)
    odd = lax.rem(segment, 2) == 1
    lane, place = lanes_of()
    pairs = base_ref.shape[0]
    blocks = base_ref.shape[2] // SUB
    rows_all = blocks * SUB
    tile = rows_all - 2 * EDGE
    rest = lax.rem(offsets_ref[0], tile)
    split = jnp.where(rotor, tile + EDGE - rest, EDGE + rest)
    shift = jnp.where(rotor, lax.rem(rows_all - rest, rows_all), rest)
    shift2 = jnp.where(rotor, tile - rest, rest + rows_all - tile)
    row_id = lax.broadcasted_iota(jnp.int32, (rows_all, LANES), 0)
    from_first = (row_id >= split) != rotor
    upper_half = lax.broadcasted_iota(jnp.int32, (rows_all, LANES), 1) >= HALF
    weight_r = rate_w * co["inv_r"]
    at_low = jnp.where(place == 0, weight_r, 0.0)
    at_high = jnp.where(place == HALF - 1, weight_r, 0.0)

    def opened(ref, k):
        halves = [divmod(k * blocks + b, 2) for b in range(blocks)]
        return jnp.concatenate(
            [ref[h] if odd_half else pltpu.roll(ref[h], HALF, 1) for h, odd_half in halves], axis=0
        )

    for b in range(blocks):
        rows = pl.ds(b * SUB, SUB)
        inside = jnp.where(odd, one_ref[rows, :], two_ref[rows, :])
        outside = jnp.where(odd, two_ref[rows, :], one_ref[rows, :])
        for a in range(pairs):
            for k in range(FIELDS):
                j = a * FIELDS + k
                moved = pltpu.roll(inside, LANES - j, 1) if j else inside
                value = base_ref[a, k, rows, :] + at_low * moved
                value = value + at_high * pltpu.roll(outside, HALF - 1 - j, 1)
                state_ref[a, k, rows, :] = value
    for k in range(FIELDS):
        mixed = jnp.where(
            from_first,
            pltpu.roll(opened(turn_ref, k), shift, 0),
            pltpu.roll(opened(turn2_ref, k), shift2, 0),
        )
        turned = jnp.where(upper_half, mixed, 0.0)
        signed = -rate_w if k == 3 else rate_w
        state_ref[pairs - 1, k] = state_ref[pairs - 1, k] + signed * turned
    write_sends(state_ref, co, segment, *sends)


def body(density, velocity, pressure, offsets):
    n_ax, n_az = lax.axis_size("ax"), lax.axis_size("az")
    planes, tile, cells = density.shape[1:]
    cycle_cells = tile * n_az

    vmem = pl.BlockSpec(memory_space=pltpu.VMEM)
    smem = pl.BlockSpec(memory_space=pltpu.SMEM)
    struct = lambda *shape: jax.ShapeDtypeStruct(shape, jnp.float32)
    tall = tile + 2 * EDGE
    block = struct(n_ax, FIELDS, tall, LANES)
    own = struct(n_ax, FIELDS, tile, LANES)
    outer_rows = struct(n_ax * FIELDS // 2, 2 * EDGE, LANES)
    up_blocks = -(-FIELDS * (tall // SUB) // 2)
    sends = (struct(up_blocks, SUB, LANES), struct(tall, LANES), struct(tall, LANES))

    def device(row, ax, az):
        return (row * n_ax + ax) * n_az + az

    every = [(row, ax, az) for row in range(2) for ax in range(n_ax) for az in range(n_az)]

    def swapped(first):
        partner = lambda x: x + 1 if (x - first) % 2 == 0 else x - 1
        return [
            (device(r, x, z), device(r, partner(x), z)) for r, x, z in every
            if 0 <= partner(x) < n_ax
        ]

    def turned(by):
        pairs = []
        for x in range(n_ax):
            for z in range(n_az):
                pairs.append((device(1, x, (z + by) % n_az), device(0, x, z)))
                pairs.append((device(0, x, z), device(1, x, (z + by) % n_az)))
        return pairs

    near = [(device(r, x, z), device(r, x, (z + (1 if r else -1)) % n_az)) for r, x, z in every]

    def call(kernel, outs, n_smem, n_vmem, scratch=(), grant=KERNEL_VMEM):
        return pl.pallas_call(
            kernel,
            out_shape=outs,
            in_specs=[smem] * n_smem + [vmem] * n_vmem,
            out_specs=jax.tree.map(lambda _: vmem, outs),
            scratch_shapes=list(scratch),
            compiler_params=pltpu.CompilerParams(vmem_limit_bytes=grant),
            cost_estimate=pl.CostEstimate(
                flops=8_000_000, bytes_accessed=3_000_000, transcendentals=0
            ),
        )

    kernel_of = lambda kernel: functools.partial(kernel, cycle_cells)
    taller = pltpu.VMEM((FIELDS, tall + SUB, LANES), jnp.float32)
    whole = pltpu.VMEM(block.shape, jnp.float32)

    chunks = call(pack_kernel, own, 0, 3, grant=None)(density[0], velocity[0], pressure[0])
    whole_tile = lax.all_to_all(chunks, "ax", 0, 0, tiled=True)

    code = 4 * ((1 - lax.axis_index("row")) * n_ax + lax.axis_index("ax"))
    code_1 = jnp.reshape(code, (1,))
    packed = offsets[0] + cycle_cells * (offsets[1] + cycle_cells * offsets[2])
    up_rows, down_rows = call(edge_kernel, (outer_rows, outer_rows), 1, 1)(code_1, whole_tile)
    up_rows = lax.ppermute(up_rows, AXES, turned(1))
    down_rows = lax.ppermute(down_rows, AXES, near)
    up_rows = lax.ppermute(up_rows, AXES, turned(0))
    start, *first = call(kernel_of(first_kernel), (block, *sends), 1, 3)(
        code_1, whole_tile, up_rows, down_rows
    )
    carry = (start, *first)

    def branch(by):
        def run(code, now, up, one, two):
            turn1 = lax.ppermute(up, AXES, turned(by))
            turn2 = lax.ppermute(up, AXES, turned((by + 1) % n_az))
            one = lax.ppermute(one, AXES, swapped(0))
            two = lax.ppermute(two, AXES, swapped(1))
            base = call(kernel_of(local_kernel), block, 1, 2, (taller, taller, whole, whole))(
                code, start, now
            )
            return base, turn1, turn2, one, two
        return run

    def substep(_, carry):
        *cells_and_edges, code, packed = carry
        index = lax.div(lax.rem(packed, cycle_cells), tile)
        code_1, left = jnp.reshape(code, (1,)), jnp.reshape(packed, (1,))
        terms = lax.switch(
            index, [branch(by) for by in range(n_az)], code_1, *cells_and_edges
        )
        state = call(kernel_of(join_kernel), (block, *sends), 2, 5)(code_1, left, *terms)
        return (*state, code + 1, lax.div(packed, cycle_cells))

    carry = (*carry, code, packed)
    carry = lax.fori_loop(0, 3, substep, carry)
    chunks = lax.all_to_all(carry[0][:, :, EDGE : EDGE + tile], "ax", 0, 0, tiled=True)
    return call(unpack_kernel, struct(FIELDS, planes, tile, cells), 0, 1)(chunks)[None]


def solution(mesh):
    placed = (
        P("row", "ax", "az", None),
        P("row", None, "ax", "az", None),
        P("row", "ax", "az", None),
        P(),
    )
    return jax.shard_map(
        body,
        mesh=mesh,
        in_specs=placed,
        out_specs=P("row", None, "ax", "az", None),
        check_vma=False,
    )
```

```python
import functools
import math

import jax
import jax.numpy as jnp
from jax import lax
from jax.experimental import pallas as pl
from jax.experimental.pallas import tpu as pltpu
from jax.sharding import PartitionSpec as P

HEAT_RATIO = 1.4
VISCOSITY = 0.8
CONDUCTION = 0.6
TIME_STEP = 0.1
AXIAL_CURVE = 4.0
AXES = ("row", "ax", "az")
FIELDS = 5
SUB = 8
LANES = 128
HALF = 64
KERNEL_VMEM = 12 * 2**20
EDGE = 4


def cell(state):
    rho, mt, mr, mz, energy = state
    inv = 1.0 / rho
    vt, vr, vz = mt * inv, mr * inv, mz * inv
    tt, rr, zz = mt * vt, mr * vr, mz * vz
    press = (HEAT_RATIO - 1.0) * (energy - 0.5 * (tt + rr + zz))
    visc = (
        None,
        VISCOSITY * vt,
        VISCOSITY * vr,
        VISCOSITY * vz,
        CONDUCTION * (press * inv),
    )
    return dict(
        mt=mt, mr=mr, mz=mz, vt=vt, vr=vr, vz=vz, tt=tt, rr=rr, zz=zz,
        tr=mt * vr, tz=mt * vz, rz=mr * vz, press=press, enth=energy + press, visc=visc,
    )


def flux_theta(c):
    return (c["mt"], c["tt"] + c["press"], c["tr"], c["tz"], c["enth"] * c["vt"])


def flux_radial(c):
    return (c["mr"], c["tr"], c["rr"] + c["press"], c["rz"], c["enth"] * c["vr"])


def flux_axial(c):
    return (c["mz"], c["tz"], c["rz"], c["zz"] + c["press"], c["enth"] * c["vz"])


def axial_terms(c):
    above, below = [], []
    for flux, visc in zip(flux_axial(c), c["visc"]):
        if visc is None:
            above.append(flux)
            below.append(-flux)
        else:
            side = AXIAL_CURVE * visc
            above.append(side + flux)
            below.append(side - flux)
    return above, below


def theta_terms(c, co):
    flux = [co["half_arc"] * f for f in flux_theta(c)]
    flux[1] = flux[1] - co["cross"] * c["visc"][2]
    flux[2] = flux[2] + co["cross"] * c["visc"][1]
    nxt, prv = [flux[0]], [-flux[0]]
    for k in range(1, FIELDS):
        side = co["arc2"] * c["visc"][k]
        nxt.append(side + flux[k])
        prv.append(side - flux[k])
    return nxt, prv


def radial_terms(c, co):
    out, inn = [], []
    for flux, visc in zip(flux_radial(c), c["visc"]):
        odd = co["half_r"] * flux
        if visc is None:
            out.append(odd)
            inn.append(-odd)
        else:
            odd = odd + 0.5 * visc
            even = co["r"] * visc
            out.append(even + odd)
            inn.append(even - odd)
    return out, inn


def wall_terms(c, half_rg, weight, sign):
    flux = flux_radial(c)
    signs = (-1.0, 1.0, 1.0, 1.0, -1.0)
    out = []
    for k in range(FIELDS):
        term = (sign * signs[k]) * (half_rg * flux[k])
        if k:
            term = term + (1.0 if k == 4 else -1.0) * (weight * c["visc"][k])
        out.append(term)
    return out


def centre_terms(c, co):
    centre = [None] + [-(co["centre"] * v) for v in c["visc"][1:]]
    centre[1] = centre[1] - co["inv_r"] * (c["tr"] + co["inv_r"] * c["visc"][1])
    centre[2] = centre[2] + co["inv_r"] * (c["tt"] + c["press"] - co["inv_r"] * c["visc"][2])
    return centre


def lanes_of():
    lane = lax.broadcasted_iota(jnp.int32, (SUB, LANES), 1)
    return lane, jnp.where(lane < HALF, lane, lane - HALF)


def coefficients(segment, cycle_cells):
    dtheta = 2.0 * math.pi / cycle_cells
    cells = (lanes_of()[1] + segment * HALF).astype(jnp.float32)
    r = cycle_cells / (2.0 * math.pi) + cells + 0.5
    inv_r = 1.0 / r
    arc2 = 1.0 / ((r * dtheta) * (r * dtheta))
    return dict(
        r=r, half_r=0.5 * r, inv_r=inv_r, half_arc=1.0 / (2.0 * r * dtheta), arc2=arc2,
        cross=1.0 / (r * r * dtheta), centre=2.0 * arc2 + 2.0 + 2.0 * AXIAL_CURVE,
    )


def weights_of(step):
    first, second = step == 0, step == 1
    old = jnp.where(first, 0.0, jnp.where(second, 0.75, 1.0 / 3.0))
    now = jnp.where(first, 1.0, jnp.where(second, 0.25, 2.0 / 3.0))
    return old, now, now * TIME_STEP


def decode(code_ref, segments):
    code = code_ref[0]
    place = lax.div(code, 4)
    return lax.rem(code, 4), lax.rem(place, segments), lax.div(place, segments) == 1


def pack_kernel(rho_ref, vel_ref, press_ref, out_ref):
    lane, _ = lanes_of()
    low = lane < HALF
    for b in range(rho_ref.shape[1] // SUB):
        rows = pl.ds(b * SUB, SUB)
        for w in range(rho_ref.shape[2] // LANES):
            cols = pl.ds(w * LANES, LANES)
            both = []
            for p in range(2):
                rho = rho_ref[p, rows, cols]
                vel = [vel_ref[d, p, rows, cols] for d in range(3)]
                square = vel[0] * vel[0] + vel[1] * vel[1] + vel[2] * vel[2]
                energy = press_ref[p, rows, cols] / (HEAT_RATIO - 1.0) + 0.5 * rho * square
                both.append([rho] + [rho * v for v in vel] + [energy])
            for k in range(FIELDS):
                first, second = both[0][k], both[1][k]
                out_ref[2 * w, k, rows, :] = jnp.where(low, first, pltpu.roll(second, HALF, 1))
                out_ref[2 * w + 1, k, rows, :] = jnp.where(low, pltpu.roll(first, HALF, 1), second)


def edge_kernel(code_ref, in_ref, up_ref, down_ref):
    front = lax.broadcasted_iota(jnp.int32, (SUB, LANES), 0) < EDGE
    _, _, rotor = decode(code_ref, in_ref.shape[0])
    end = pl.ds(in_ref.shape[2] - SUB, SUB)
    for i in range(up_ref.shape[0]):
        one, two = divmod(2 * i, FIELDS), divmod(2 * i + 1, FIELDS)
        head = jnp.where(
            front, in_ref[*one, pl.ds(0, SUB), :], pltpu.roll(in_ref[*two, pl.ds(0, SUB), :], EDGE, 0)
        )
        tail = jnp.where(front, pltpu.roll(in_ref[*one, end, :], EDGE, 0), in_ref[*two, end, :])
        up_ref[i] = jnp.where(rotor, tail, head)
        down_ref[i] = jnp.where(rotor, head, tail)


def unpack_kernel(in_ref, out_ref):
    lane, _ = lanes_of()
    low = lane < HALF
    for b in range(out_ref.shape[2] // SUB):
        rows = pl.ds(b * SUB, SUB)
        for w in range(in_ref.shape[0] // 2):
            cols = pl.ds(w * LANES, LANES)
            for k in range(FIELDS):
                inner, outer = in_ref[2 * w, k, rows, :], in_ref[2 * w + 1, k, rows, :]
                out_ref[k, 0, rows, cols] = jnp.where(low, inner, pltpu.roll(outer, HALF, 1))
                out_ref[k, 1, rows, cols] = jnp.where(low, pltpu.roll(inner, HALF, 1), outer)


def write_sends(state_ref, co, segment, up_ref, one_ref, two_ref):
    odd = lax.rem(segment, 2) == 1
    lane, place = lanes_of()
    pairs = state_ref.shape[0]
    blocks = state_ref.shape[2] // SUB
    top = []
    for b in range(blocks):
        rows = pl.ds(b * SUB, SUB)
        packed_out = jnp.zeros((SUB, LANES), jnp.float32)
        packed_in = jnp.zeros((SUB, LANES), jnp.float32)
        for a in range(pairs):
            c = cell([state_ref[a, k, rows, :] for k in range(FIELDS)])
            to_out, to_in = radial_terms(c, co)
            for k in range(FIELDS):
                j = a * FIELDS + k
                here = place == j
                moved = pltpu.roll(to_out[k], (j + 1 - HALF) % LANES, 1)
                packed_out = jnp.where(here, moved, packed_out)
                moved = pltpu.roll(to_in[k], j, 1) if j else to_in[k]
                packed_in = jnp.where(here, moved, packed_in)
            if a == pairs - 1:
                top.append(axial_terms(c)[0])
        one_ref[rows, :] = jnp.where(odd, packed_in, packed_out)
        two_ref[rows, :] = jnp.where(odd, packed_out, packed_in)
    halves = [top[b][k] for k in range(FIELDS) for b in range(blocks)]
    for h in range(up_ref.shape[0]):
        value = pltpu.roll(halves[2 * h], HALF, 1)
        if 2 * h + 1 < len(halves):
            value = jnp.where(lane < HALF, value, halves[2 * h + 1])
        up_ref[h] = value


def first_kernel(cycle_cells, code_ref, in_ref, one_ref, two_ref, state_ref, *sends):
    _, segment, rotor = decode(code_ref, in_ref.shape[0])
    rows = in_ref.shape[2]
    for a in range(in_ref.shape[0]):
        for k in range(FIELDS):
            i, half = divmod(a * FIELDS + k, 2)
            half = pl.ds(half * EDGE, EDGE)
            one, two = one_ref[i, half, :], two_ref[i, half, :]
            state_ref[a, k, pl.ds(0, EDGE), :] = jnp.where(rotor, one, two)
            state_ref[a, k, pl.ds(EDGE, rows), :] = in_ref[a, k]
            state_ref[a, k, pl.ds(EDGE + rows, EDGE), :] = jnp.where(rotor, two, one)
    co = coefficients(segment, cycle_cells)
    write_sends(state_ref, co, segment, *sends)


def local_kernel(cycle_cells, code_ref, old_ref, now_ref, base_ref, nxt_s, prv_s, up_s, dn_s):
    segments = now_ref.shape[0]
    step, segment, _ = decode(code_ref, segments)
    co = coefficients(segment, cycle_cells)
    lane, place = lanes_of()
    low = lane < HALF
    pairs = now_ref.shape[0]
    blocks = now_ref.shape[2] // SUB
    at_inner, at_outer = segment == 0, segment == segments - 1
    is_inner, is_outer = place == 0, place == HALF - 1
    low_half, low_weight = 0.5 * (co["r"] - 1.0), co["r"] - 0.5
    high_half, high_weight = 0.5 * (co["r"] + 1.0), co["r"] + 0.5
    zero = jnp.zeros((SUB, LANES), jnp.float32)
    low_half = jnp.where(at_inner, low_half, zero)
    low_weight = jnp.where(at_inner, low_weight, zero)
    high_half = jnp.where(at_outer, high_half, zero)
    high_weight = jnp.where(at_outer, high_weight, zero)
    rows_end = blocks * SUB
    for k in range(FIELDS):
        nxt_s[k, pl.ds(0, SUB), :] = zero
        prv_s[k, pl.ds(rows_end, SUB), :] = zero

    def pair(a, carry):
        for b in range(blocks):
            rows = pl.ds(b * SUB, SUB)
            c = cell([now_ref[a, k, rows, :] for k in range(FIELDS)])
            to_out, to_in = radial_terms(c, co)
            inner = wall_terms(c, low_half, low_weight, 1.0)
            outer = wall_terms(c, high_half, high_weight, -1.0)
            centre = centre_terms(c, co)
            nxt, prv = theta_terms(c, co)
            above, below = axial_terms(c)
            for k in range(FIELDS):
                inside = jnp.where(is_inner, inner[k], pltpu.roll(to_out[k], 1, 1))
                outside = jnp.where(is_outer, outer[k], pltpu.roll(to_in[k], LANES - 1, 1))
                total = co["inv_r"] * (inside + outside)
                if centre[k] is not None:
                    total = total + centre[k]
                nxt_s[k, pl.ds(b * SUB + SUB, SUB), :] = nxt[k]
                prv_s[k, rows, :] = prv[k]
                swapped_up = pltpu.roll(above[k], HALF, 1)
                swapped_dn = pltpu.roll(below[k], HALF, 1)
                total = total + jnp.where(low, swapped_dn, swapped_up)
                base_ref[a, k, rows, :] = total
                up_s[a, k, rows, :] = swapped_up
                dn_s[a, k, rows, :] = swapped_dn
        for b in range(blocks):
            rows = pl.ds(b * SUB, SUB)
            for k in range(FIELDS):
                base_ref[a, k, rows, :] = (
                    base_ref[a, k, rows, :]
                    + nxt_s[k, pl.ds(b * SUB + SUB - 1, SUB), :]
                    + prv_s[k, pl.ds(b * SUB + 1, SUB), :]
                )
        return carry

    lax.fori_loop(0, pairs, pair, 0)
    old_w, now_w, rate_w = weights_of(step)

    def finish(a, carry):
        lower = jnp.maximum(a - 1, 0)
        upper = jnp.minimum(a + 1, pairs - 1)
        has_upper = a < pairs - 1
        first = a == 0
        for b in range(blocks):
            rows = pl.ds(b * SUB, SUB)
            for k in range(FIELDS):
                from_below = up_s[lower, k, rows, :]
                from_below = jnp.where(first, pltpu.roll(from_below, HALF, 1), from_below)
                from_above = jnp.where(has_upper, dn_s[upper, k, rows, :], zero)
                rate = base_ref[a, k, rows, :] + jnp.where(low, from_below, from_above)
                base_ref[a, k, rows, :] = (
                    old_w * old_ref[a, k, rows, :] + now_w * now_ref[a, k, rows, :] + rate_w * rate
                )
        return carry

    lax.fori_loop(0, pairs, finish, 0)


def join_kernel(cycle_cells, code_ref, offsets_ref, base_ref, turn_ref, turn2_ref, one_ref,
                two_ref, state_ref, *sends):
    step, segment, rotor = decode(code_ref, base_ref.shape[0])
    co = coefficients(segment, cycle_cells)
    _, _, rate_w = weights_of(step)
    odd = lax.rem(segment, 2) == 1
    lane, place = lanes_of()
    pairs = base_ref.shape[0]
    blocks = base_ref.shape[2] // SUB
    rows_all = blocks * SUB
    tile = rows_all - 2 * EDGE
    rest = lax.rem(offsets_ref[0], tile)
    split = jnp.where(rotor, tile + EDGE - rest, EDGE + rest)
    shift = jnp.where(rotor, lax.rem(rows_all - rest, rows_all), rest)
    shift2 = jnp.where(rotor, tile - rest, rest + rows_all - tile)
    row_id = lax.broadcasted_iota(jnp.int32, (rows_all, LANES), 0)
    from_first = (row_id >= split) != rotor
    upper_half = lax.broadcasted_iota(jnp.int32, (rows_all, LANES), 1) >= HALF
    weight_r = rate_w * co["inv_r"]
    at_low = jnp.where(place == 0, weight_r, 0.0)
    at_high = jnp.where(place == HALF - 1, weight_r, 0.0)

    def opened(ref, k):
        halves = [divmod(k * blocks + b, 2) for b in range(blocks)]
        return jnp.concatenate(
            [ref[h] if odd_half else pltpu.roll(ref[h], HALF, 1) for h, odd_half in halves], axis=0
        )

    for b in range(blocks):
        rows = pl.ds(b * SUB, SUB)
        inside = jnp.where(odd, one_ref[rows, :], two_ref[rows, :])
        outside = jnp.where(odd, two_ref[rows, :], one_ref[rows, :])
        for a in range(pairs):
            for k in range(FIELDS):
                j = a * FIELDS + k
                moved = pltpu.roll(inside, LANES - j, 1) if j else inside
                value = base_ref[a, k, rows, :] + at_low * moved
                value = value + at_high * pltpu.roll(outside, HALF - 1 - j, 1)
                state_ref[a, k, rows, :] = value
    for k in range(FIELDS):
        mixed = jnp.where(
            from_first,
            pltpu.roll(opened(turn_ref, k), shift, 0),
            pltpu.roll(opened(turn2_ref, k), shift2, 0),
        )
        turned = jnp.where(upper_half, mixed, 0.0)
        signed = -rate_w if k == 3 else rate_w
        state_ref[pairs - 1, k] = state_ref[pairs - 1, k] + signed * turned
    if sends:
        write_sends(state_ref, co, segment, *sends)


def body(density, velocity, pressure, offsets):
    n_ax, n_az = lax.axis_size("ax"), lax.axis_size("az")
    planes, tile, cells = density.shape[1:]
    cycle_cells = tile * n_az

    vmem = pl.BlockSpec(memory_space=pltpu.VMEM)
    smem = pl.BlockSpec(memory_space=pltpu.SMEM)
    struct = lambda *shape: jax.ShapeDtypeStruct(shape, jnp.float32)
    tall = tile + 2 * EDGE
    block = struct(n_ax, FIELDS, tall, LANES)
    own = struct(n_ax, FIELDS, tile, LANES)
    outer_rows = struct(n_ax * FIELDS // 2, 2 * EDGE, LANES)
    up_blocks = -(-FIELDS * (tall // SUB) // 2)
    sends = (struct(up_blocks, SUB, LANES), struct(tall, LANES), struct(tall, LANES))

    def device(row, ax, az):
        return (row * n_ax + ax) * n_az + az

    every = [(row, ax, az) for row in range(2) for ax in range(n_ax) for az in range(n_az)]

    def swapped(first):
        partner = lambda x: x + 1 if (x - first) % 2 == 0 else x - 1
        return [
            (device(r, x, z), device(r, partner(x), z)) for r, x, z in every
            if 0 <= partner(x) < n_ax
        ]

    def turned(by):
        pairs = []
        for x in range(n_ax):
            for z in range(n_az):
                pairs.append((device(1, x, (z + by) % n_az), device(0, x, z)))
                pairs.append((device(0, x, z), device(1, x, (z + by) % n_az)))
        return pairs

    near = [(device(r, x, z), device(r, x, (z + (1 if r else -1)) % n_az)) for r, x, z in every]

    def call(kernel, outs, n_smem, n_vmem, scratch=(), grant=KERNEL_VMEM):
        return pl.pallas_call(
            kernel,
            out_shape=outs,
            in_specs=[smem] * n_smem + [vmem] * n_vmem,
            out_specs=jax.tree.map(lambda _: vmem, outs),
            scratch_shapes=list(scratch),
            compiler_params=pltpu.CompilerParams(vmem_limit_bytes=grant),
            cost_estimate=pl.CostEstimate(
                flops=8_000_000, bytes_accessed=3_000_000, transcendentals=0
            ),
        )

    kernel_of = lambda kernel: functools.partial(kernel, cycle_cells)
    taller = pltpu.VMEM((FIELDS, tall + SUB, LANES), jnp.float32)
    whole = pltpu.VMEM(block.shape, jnp.float32)

    chunks = call(pack_kernel, own, 0, 3, grant=None)(density[0], velocity[0], pressure[0])
    whole_tile = lax.all_to_all(chunks, "ax", 0, 0, tiled=True)

    code = 4 * ((1 - lax.axis_index("row")) * n_ax + lax.axis_index("ax"))
    code_1 = jnp.reshape(code, (1,))
    packed = offsets[0] + cycle_cells * (offsets[1] + cycle_cells * offsets[2])
    up_rows, down_rows = call(edge_kernel, (outer_rows, outer_rows), 1, 1)(code_1, whole_tile)
    up_rows = lax.ppermute(up_rows, AXES, turned(1))
    down_rows = lax.ppermute(down_rows, AXES, near)
    up_rows = lax.ppermute(up_rows, AXES, turned(0))
    start, *first = call(kernel_of(first_kernel), (block, *sends), 1, 3)(
        code_1, whole_tile, up_rows, down_rows
    )
    carry = (start, *first)

    def branch(by):
        def run(code, now, up, one, two):
            turn1 = lax.ppermute(up, AXES, turned(by))
            turn2 = lax.ppermute(up, AXES, turned((by + 1) % n_az))
            one = lax.ppermute(one, AXES, swapped(0))
            two = lax.ppermute(two, AXES, swapped(1))
            base = call(kernel_of(local_kernel), block, 1, 2, (taller, taller, whole, whole))(
                code, start, now
            )
            return base, turn1, turn2, one, two
        return run

    def substep(_, carry):
        *cells_and_edges, code, packed = carry
        index = lax.div(lax.rem(packed, cycle_cells), tile)
        code_1, left = jnp.reshape(code, (1,)), jnp.reshape(packed, (1,))
        terms = lax.switch(
            index, [branch(by) for by in range(n_az)], code_1, *cells_and_edges
        )

        def usual(*operands):
            return tuple(call(kernel_of(join_kernel), (block, *sends), 2, 5)(*operands))

        def final(*operands):
            state, = call(kernel_of(join_kernel), (block,), 2, 5)(*operands)
            return (state, *cells_and_edges[1:])

        state = lax.cond(lax.rem(code, 4) == 2, final, usual, code_1, left, *terms)
        return (*state, code + 1, lax.div(packed, cycle_cells))

    carry = (*carry, code, packed)
    carry = lax.fori_loop(0, 3, substep, carry)
    chunks = lax.all_to_all(carry[0][:, :, EDGE : EDGE + tile], "ax", 0, 0, tiled=True)
    return call(unpack_kernel, struct(FIELDS, planes, tile, cells), 0, 1)(chunks)[None]


def solution(mesh):
    placed = (
        P("row", "ax", "az", None),
        P("row", None, "ax", "az", None),
        P("row", "ax", "az", None),
        P(),
    )
    return jax.shard_map(
        body,
        mesh=mesh,
        in_specs=placed,
        out_specs=P("row", None, "ax", "az", None),
        check_vma=False,
    )
```
